32 devices in a mesh: gx: 4 (over y, core), yz: 8 (over z, x).
Axes of the slice: x: 2, y: 2, z: 4, core: 2. Of those that a mesh axis runs over, the one named last changes fastest.
Arguments:
- composition: float32 [4096, 20, 128], P(('gx', 'yz')), may hold values from -6 to 6
- particle_mass: float32 [4096, 128], P(('gx', 'yz')), may hold values from 0.5 to 2
- mixing_rate: float32 [4096, 128], P(('gx', 'yz')), may hold values from 0.2 to 3
- cell_index: int32 [4096, 128], P(('gx', 'yz')), may hold values from 0 to 4095, as said below
- section_counts: int32 [4096], P(('gx', 'yz')), may hold values from 1 to 6, as said below
- block_shuffle: int32 [32, 128], P(('gx', 'yz')), may hold values from 0 to 127, as said below
- batch_inverse: float32 [32, 20, 20], P(('gx', 'yz')), may hold values from -1.25 to 1.25
- rate_exponents: float32 [84, 20], replicated, may hold values from -1.25 to 1.25
- stoichiometry: float32 [20, 84], replicated, may hold values from -0.625 to 0.625
Outputs:
- reacted: float32 [4096, 20, 128], P(('gx', 'yz'))
The draws below stay inside these ranges and needn't reach their ends.
Inputs may be any that keep to these rules, and one draw needn't show every extreme that they name: `cell_index`: A particle of the device at index i of gx and j of yz (d = i * 8 + j) lies in slab i - 1, i or i + 1, slab s holding cells s * 128 * 8 to (s + 1) * 128 * 8 - 1; that device's first 128 particles lie one each in cells d * 128 to d * 128 + 127. `section_counts`: some block has exactly 6 sections. `block_shuffle`: each row is a permutation of 0 to 127.
All inputs are finite; a program needn't handle non-finite values.
Results may differ from the reference program's by a relative error of at most 0.0011.
Values sent between devices are 32-bit elements; how exact they have to be, the bound alone decides.
No kernel may reach another device: no remote copies, remote signals or barrier semaphores. Data moves between devices by JAX's collectives and lax.ppermute only.
A program may use at most 128 MiB of HBM per device.

```python
import math
import jax
import jax.numpy as jnp
from jax import lax

NS = 20
NR = 84
BLK = 128
SMAX = 6
BLOCKS_DEV = 128
CELL_DEV = 128
BLOCKS = 4096
CELLS = 4096
N_GX = 4
N_YZ = 8
DEVICES = 32


def draw_cell_index(key, part):
    per_device = BLOCKS_DEV * BLK
    slab_cells = CELL_DEV * N_YZ
    device = jnp.arange(DEVICES, dtype=jnp.int32)[:, None]
    slab_row = device // N_YZ
    first_key, second_key = jax.random.split(jax.random.fold_in(key, 11), 2)
    choose = jax.random.randint(first_key, (DEVICES, per_device), 0, 4)
    offset = jnp.where(choose == 0, -1, jnp.where(choose == 3, 1, 0))
    target = jnp.clip(slab_row + offset, 0, N_GX - 1)
    inside = jax.random.randint(second_key, (DEVICES, per_device), 0, slab_cells)
    placed = target * slab_cells + inside
    lane_index = jnp.arange(per_device, dtype=jnp.int32)[None, :]
    owned = device * CELL_DEV + lane_index
    placed = jnp.where(lane_index < CELL_DEV, owned, placed)
    return placed.reshape(BLOCKS, BLK).astype(jnp.int32)


def draw_section_counts(key, part):
    first_key, second_key, third_key = jax.random.split(jax.random.fold_in(key, 23), 3)
    level = jax.random.randint(first_key, (DEVICES, 1), 0, 3)
    ceiling = jnp.where(level == 0, 2, jnp.where(level == 1, 4, SMAX))
    drawn = jax.random.randint(second_key, (DEVICES, BLOCKS_DEV), 0, 1 << 20)
    counts = (1 + drawn % ceiling).reshape(-1)
    picked = jax.random.randint(third_key, (), 0, BLOCKS)
    counts = jnp.where(jnp.arange(BLOCKS) == picked, SMAX, counts)
    return counts.astype(jnp.int32)


def draw_block_shuffle(key, part):
    base = jnp.broadcast_to(jnp.arange(BLOCKS_DEV, dtype=jnp.int32), (DEVICES, BLOCKS_DEV))
    return jax.random.permutation(jax.random.fold_in(key, 37), base, axis=1, independent=True).astype(jnp.int32)


def levels(stream_key, extent, cuts, smallest, largest):
    loudness, own = 1.0, jax.random.fold_in(stream_key, 6)
    for axis_at, shards_of in cuts:
        steps = jnp.exp(jax.random.uniform(jax.random.fold_in(own, axis_at), (shards_of,), jnp.float32, smallest / len(cuts), largest / len(cuts)))
        loudness = loudness * jnp.repeat(steps, extent[axis_at] // shards_of).reshape([-1 if axis == axis_at else 1 for axis in range(len(extent))])
    return loudness


def scatter_about(key, extent, spread, bound, cuts=(), kind=jnp.bfloat16):
    array = jax.random.normal(key, extent, jnp.float32) * spread
    if len(cuts) > 0:
        array = levels(key, extent, cuts, -0.22, 0.18) * array
    return jnp.clip(array, min=-bound, max=bound).astype(kind)


def setup_inputs(seed: int = 0) -> dict:
    key_of = jax.random.split(jax.random.key(seed), 10)
    composition = scatter_about(key_of[0], (BLOCKS, NS, BLK), 1.0, 6.0, ((0, 32),), jnp.float32)
    particle_mass = jnp.clip(jnp.exp(math.log(2.0) - 1.3862944 * jax.random.uniform(key_of[1], (BLOCKS, BLK), jnp.float32) ** levels(key_of[1], (BLOCKS, BLK), ((0, 32),), -0.2, 0.2)), 0.5, 2.0)
    mixing_rate = jnp.clip(jnp.exp(math.log(3.0) - 2.7080502 * jax.random.uniform(key_of[2], (BLOCKS, BLK), jnp.float32) ** levels(key_of[2], (BLOCKS, BLK), ((0, 32),), -0.2, 0.2)), 0.2, 3.0)
    cell_index = draw_cell_index(jax.random.fold_in(key_of[9], 71), 0)
    section_counts = draw_section_counts(jax.random.fold_in(key_of[9], 71), 0)
    block_shuffle = draw_block_shuffle(jax.random.fold_in(key_of[9], 71), 0)
    batch_inverse = scatter_about(key_of[6], (DEVICES, NS, NS), NS ** -0.5, 1.25, ((0, 32),), jnp.float32)
    rate_exponents = scatter_about(key_of[7], (NR, NS), NS ** -0.5, 1.25, (), jnp.float32)
    stoichiometry = scatter_about(key_of[8], (NS, NR), NR ** -0.5, 0.625, (), jnp.float32)
    return {"composition": composition, "particle_mass": particle_mass, "mixing_rate": mixing_rate, "cell_index": cell_index, "section_counts": section_counts, "block_shuffle": block_shuffle, "batch_inverse": batch_inverse, "rate_exponents": rate_exponents, "stoichiometry": stoichiometry}


step_size = 0.25


def section_update(current, matrices, rate_exponents, stoichiometry):
    progress = jnp.tanh(jnp.einsum('rj,bjk->brk', rate_exponents, current, precision=lax.Precision.HIGHEST))
    forcing = jnp.einsum('ir,brk->bik', stoichiometry, progress, precision=lax.Precision.HIGHEST)
    return jnp.einsum('bij,bjk->bik', matrices, forcing, precision=lax.Precision.HIGHEST)


def reference(composition, particle_mass, mixing_rate, cell_index, section_counts, block_shuffle, batch_inverse, rate_exponents, stoichiometry):
    flat_cell = cell_index.reshape(-1)
    weighted = jnp.moveaxis(composition * particle_mass[:, None, :], 1, 0).reshape(NS, -1)
    cell_sum = jnp.zeros((NS, CELLS), jnp.float32).at[:, flat_cell].add(weighted)
    cell_mass = jnp.zeros((CELLS,), jnp.float32).at[flat_cell].add(particle_mass.reshape(-1))
    cell_means = cell_sum / cell_mass[None, :]
    looked = jnp.moveaxis(cell_means[:, flat_cell].reshape(NS, BLOCKS, BLK), 0, 1)
    mixed_state = looked + (composition - looked) * jnp.exp(-mixing_rate)[:, None, :]
    slot_of = jnp.argsort(block_shuffle, axis=1, stable=True)
    batch_of = (slot_of // (BLOCKS_DEV // DEVICES)).reshape(-1)
    group = 64
    groups = BLOCKS // group
    grouped_state = mixed_state.reshape(groups, group, NS, BLK)
    grouped_batch = batch_of.reshape(groups, group)
    grouped_counts = section_counts.reshape(groups, group)

    def one_group(inputs):
        current, batches, counts = inputs
        matrices = batch_inverse[batches]
        for section_index in range(SMAX):
            updated = current + step_size * section_update(current, matrices, rate_exponents, stoichiometry)
            current = jnp.where((counts > section_index)[:, None, None], updated, current)
        return current

    result = lax.map(one_group, (grouped_state, grouped_batch, grouped_counts))
    return result.reshape(BLOCKS, NS, BLK)
```

```python
import functools

import jax
import jax.numpy as jnp
from jax import lax
from jax.experimental import pallas as pl
from jax.experimental.pallas import tpu as pltpu
from jax.sharding import PartitionSpec as P


STEP = 0.25
CELL_DEV = 128
LOW = 256
BF16 = jnp.bfloat16
F32 = jnp.float32


def round_up(value, multiple):
    return -(-value // multiple) * multiple


def moments_kernel(place_ref, comp_ref, mass_ref, cell_ref, out_ref, acc_ref, *, high, rows):
    step = pl.program_id(0)
    species, step_blocks, lanes = comp_ref.shape
    flat = comp_ref.reshape(species * step_blocks, lanes)

    @pl.when(step == 0)
    def _():
        acc_ref[...] = jnp.zeros_like(acc_ref)

    iota_low = lax.broadcasted_iota(jnp.int32, (LOW, lanes), 0).astype(F32).astype(BF16)
    local = cell_ref[...] - place_ref[0]
    hi = (local // LOW).astype(F32)
    lo = (local % LOW).astype(F32)
    zeros = jnp.zeros((rows - species - 1, lanes), F32)
    tables, spreads = [], []
    for b in range(step_blocks):
        m = mass_ref[b : b + 1, :]
        w = flat[pl.ds(b, species, stride=step_blocks), :] * m
        v = jnp.concatenate([w, m, zeros], axis=0)
        upper = v.astype(BF16).astype(F32)
        pieces = jnp.concatenate([upper, v - upper], axis=0).astype(BF16)
        low_row = jnp.broadcast_to(lo[b : b + 1, :], (LOW, lanes)).astype(BF16)
        tables.append(jnp.where(low_row == iota_low, BF16(1), BF16(0)))
        high_row = jnp.broadcast_to(hi[b : b + 1, :], (2 * rows, lanes)).astype(BF16)
        spreads.append(
            jnp.concatenate(
                [jnp.where(high_row == BF16(h), pieces, BF16(0)) for h in range(high)], axis=0
            )
        )
    table = jnp.concatenate(tables, axis=1)
    spread = jnp.concatenate(spreads, axis=1)
    acc_ref[...] += lax.dot_general(
        spread, table, (((1,), (1,)), ((), ())), preferred_element_type=F32
    )

    @pl.when(step == pl.num_programs(0) - 1)
    def _():
        per = high // 3
        for h in range(high):
            top = h * 2 * rows
            total = acc_ref[top : top + rows, :] + acc_ref[top + rows : top + 2 * rows, :]
            slab = h // per
            slot = 0 if slab == 1 else place_ref[1 + slab // 2]
            out_ref[slot, :, (h % per) * LOW : (h % per + 1) * LOW] = total


def moments(place, comp, mass, cell, slab_cells, rows):
    species, blocks, lanes = comp.shape
    high = 3 * slab_cells // LOW
    step_blocks = min(32, blocks)
    return pl.pallas_call(
        functools.partial(moments_kernel, high=high, rows=rows),
        out_shape=jax.ShapeDtypeStruct((3, rows, slab_cells), F32),
        grid_spec=pltpu.PrefetchScalarGridSpec(
            num_scalar_prefetch=1,
            grid=(blocks // step_blocks,),
            in_specs=[
                pl.BlockSpec((species, step_blocks, lanes), lambda s, p: (0, s, 0)),
                pl.BlockSpec((step_blocks, lanes), lambda s, p: (s, 0)),
                pl.BlockSpec((step_blocks, lanes), lambda s, p: (s, 0)),
            ],
            out_specs=pl.BlockSpec((3, rows, slab_cells), lambda s, p: (0, 0, 0)),
            scratch_shapes=[pltpu.VMEM((2 * rows * high, LOW), F32)],
        ),
        compiler_params=pltpu.CompilerParams(vmem_limit_bytes=48 << 20),
        cost_estimate=pl.CostEstimate(
            flops=2 * blocks * lanes * high * LOW * 2 * rows, bytes_accessed=4 * comp.size, transcendentals=0
        ),
        name="moments",
    )(place, comp, mass, cell)


def react_kernel(
    order_ref, count_ref, batch_ref, place_ref,
    own_ref, near_ref, far_ref, comp_ref, rate_ref, cell_ref, rates_ref, net_ref,
    out_ref, table_ref, net_pack_ref, *, group,
):
    species, blocks, lanes = comp_ref.shape
    rows, slab_cells = own_ref.shape
    steps = rates_ref.shape[0]
    flat = comp_ref.reshape(species * blocks, lanes)
    out_flat = out_ref.reshape(species * blocks, lanes)
    per = slab_cells // LOW
    high = 3 * per
    first = place_ref[0]
    left_near = place_ref[1] == 1
    keep = lax.broadcasted_iota(jnp.int32, (rows, LOW), 0) < species

    for h in range(high):
        slab, cols = h // per, slice((h % per) * LOW, (h % per + 1) * LOW)
        if slab == 1:
            t = own_ref[:, cols]
        elif slab == 0:
            t = jnp.where(left_near, near_ref[:, cols], far_ref[:, cols])
        else:
            t = jnp.where(left_near, far_ref[:, cols], near_ref[:, cols])
        m = t[species : species + 1, :]
        mean = jnp.where(keep & (m > 0), t / m, 0.0)
        upper = mean.astype(BF16).astype(F32)
        table_ref[h * rows : (h + 1) * rows, :LOW] = upper
        table_ref[h * rows : (h + 1) * rows, LOW:] = mean - upper

    iota_low = lax.broadcasted_iota(jnp.int32, (LOW, lanes), 0).astype(F32).astype(BF16)
    zeros = jnp.zeros((rows - species, lanes), F32)
    width = group * lanes
    magic = jnp.float32(49152.0)

    def one_group(g, carry):
        base = g * group
        ids = [order_ref[base + j] for j in range(group)]
        hots, his = [], []
        for j in range(group):
            local = cell_ref[pl.ds(ids[j], 1), :] - first
            low_row = jnp.broadcast_to((local % LOW).astype(F32), (LOW, lanes)).astype(BF16)
            his.append(local // LOW)
            hots.append(jnp.where(low_row == iota_low, BF16(1), BF16(0)))
        hot = jnp.concatenate(hots, axis=1)
        hot = jnp.concatenate([hot, hot], axis=0)
        picked = jnp.dot(table_ref[...].astype(BF16), hot, preferred_element_type=F32)
        xs = []
        for j in range(group):
            part = slice(j * lanes, (j + 1) * lanes)
            high_row = jnp.broadcast_to(his[j], (rows, lanes))
            looked = jnp.where(high_row == 0, picked[0:rows, part], 0.0)
            for h in range(1, high):
                looked = jnp.where(high_row == h, picked[h * rows : (h + 1) * rows, part], looked)
            decay = jnp.exp(-rate_ref[pl.ds(ids[j], 1), :])
            c = jnp.concatenate([flat[pl.ds(ids[j], species, stride=blocks), :], zeros], axis=0)
            xs.append(looked + (c - looked) * decay)
        x = jnp.concatenate(xs, axis=1)
        for p in range(group // 2):
            net_pack_ref[p] = jnp.concatenate(
                [net_ref[batch_ref[base + 2 * p]], net_ref[batch_ref[base + 2 * p + 1]]], axis=0
            ).astype(BF16)
        counts = [count_ref[base + j] for j in range(group)]

        def section(s, x):
            xh = x.astype(BF16).astype(F32)
            k1 = jnp.concatenate([xh, x - xh, xh, jnp.zeros((8, width), F32)], axis=0).astype(BF16)
            t = jnp.tanh(jnp.dot(rates_ref[...], k1, preferred_element_type=F32))
            th = (t + magic) - magic
            k2 = jnp.concatenate([th, t - th, th[: LOW - 2 * steps]], axis=0).astype(BF16)
            new = []
            for p in range(group // 2):
                f = jnp.dot(
                    net_pack_ref[p], k2[:, 2 * p * lanes : 2 * (p + 1) * lanes], preferred_element_type=F32
                )
                for i in range(2):
                    j = 2 * p + i
                    scale = jnp.where(counts[j] > s, STEP, 0.0).astype(F32)
                    new.append(
                        x[:, j * lanes : (j + 1) * lanes]
                        + scale * f[rows * i : rows * (i + 1), i * lanes : (i + 1) * lanes]
                    )
            return jnp.concatenate(new, axis=1)

        x = lax.fori_loop(0, counts[0], section, x)
        for j in range(group):
            out_flat[pl.ds(ids[j], species, stride=blocks), :] = x[:species, j * lanes : (j + 1) * lanes]
        return carry

    lax.fori_loop(0, blocks // group, one_group, 0)


def react(order, counts, batch, place, own, near, far, comp, rate, cell, rates, net):
    species, blocks, lanes = comp.shape
    rows, slab_cells = own.shape
    high = 3 * slab_cells // LOW
    group = min(16, blocks)
    vmem = pl.BlockSpec(memory_space=pltpu.VMEM)
    return pl.pallas_call(
        functools.partial(react_kernel, group=group),
        out_shape=jax.ShapeDtypeStruct(comp.shape, F32),
        grid_spec=pltpu.PrefetchScalarGridSpec(
            num_scalar_prefetch=4,
            grid=(),
            in_specs=[vmem] * 8,
            out_specs=vmem,
            scratch_shapes=[
                pltpu.VMEM((rows * high, 2 * LOW), F32),
                pltpu.VMEM((group // 2, 2 * rows, LOW), BF16),
            ],
        ),
        compiler_params=pltpu.CompilerParams(vmem_limit_bytes=56 << 20),
        cost_estimate=pl.CostEstimate(
            flops=2 * blocks * lanes * high * LOW * 2 * rows, bytes_accessed=8 * comp.size, transcendentals=0
        ),
        name="react",
    )(order, counts, batch, place, own, near, far, comp, rate, cell, rates, net)


def split_two(values):
    upper = lax.reduce_precision(values, 8, 7)
    return upper, lax.reduce_precision(values - upper, 8, 7)


def pack_rates(rates, rows, steps):
    reactions, species = rates.shape
    extra = steps - reactions
    start = LOW - 2 * steps
    doubled = jnp.concatenate([rates, rates[start : start + extra]], axis=0)
    doubled = jnp.pad(doubled, ((0, 0), (0, rows - species)))
    upper, lower = split_two(doubled)
    return jnp.concatenate([upper, upper, lower, jnp.zeros((steps, 8), F32)], axis=1).astype(BF16)


def pack_net(inverse, stoichiometry, rows, steps):
    batches, species, _ = inverse.shape
    reactions = stoichiometry.shape[1]
    net = jnp.einsum("qij,jr->qir", inverse, stoichiometry, precision=lax.Precision.HIGHEST)
    upper, lower = split_two(net)
    start = LOW - 2 * steps
    zeros = jnp.zeros((batches, species, steps - reactions), F32)
    full = jnp.concatenate(
        [upper, lower[:, :, start:], upper, zeros, lower[:, :, :start]], axis=2
    )
    return jnp.pad(full, ((0, 0), (0, rows - species), (0, 0)))


def gather_inverse(inverse, devices):
    species = inverse.shape[-1]
    size = species * species
    flat = jnp.pad(inverse.reshape(size), (0, round_up(size, 128) - size)).reshape(-1, 128)
    sent = jnp.broadcast_to(flat[None], (devices,) + flat.shape)
    got = lax.all_to_all(sent, ("gx", "yz"), split_axis=0, concat_axis=0, tiled=True)
    return got.reshape(devices, -1)[:, :size].reshape(devices, species, species)


def swap_pairs(near, far):
    count = lax.axis_size("gx")
    first = [(i, i ^ 1) for i in range(count) if i ^ 1 < count]
    second = [(i, i - 1 if i % 2 == 0 else i + 1) for i in range(count)]
    second = [(i, j) for i, j in second if 0 <= j < count]
    return lax.ppermute(near, "gx", first), lax.ppermute(far, "gx", second)


def local(
    composition, particle_mass, mixing_rate, cell_index, section_counts, block_shuffle,
    batch_inverse, rate_exponents, stoichiometry,
):
    blocks, species, lanes = composition.shape
    reactions = rate_exponents.shape[0]
    columns = lax.axis_size("yz")
    devices = lax.axis_size("gx") * columns
    slab_cells = CELL_DEV * columns
    rows = round_up(species + 1, 8)
    steps = round_up(reactions, 8)
    slab = lax.axis_index("gx")
    odd = slab % 2
    place = jnp.stack([(slab - 1) * slab_cells, 2 - odd, 1 + odd]).astype(jnp.int32)

    inverses = gather_inverse(batch_inverse[0], devices)
    comp = jnp.transpose(composition, (1, 0, 2))
    partial = moments(place, comp, particle_mass, cell_index, slab_cells, rows)
    got_near, got_far = swap_pairs(partial[1], partial[2])
    own = partial[0] + got_near + got_far
    distance = 1
    while distance < columns:
        own = own + lax.ppermute(own, "yz", [(i, i ^ distance) for i in range(columns)])
        distance *= 2
    near, far = swap_pairs(own, own)

    block_ids = jnp.arange(blocks, dtype=jnp.int32)
    ahead = (section_counts[None, :] > section_counts[:, None]) | (
        (section_counts[None, :] == section_counts[:, None]) & (block_ids[None, :] < block_ids[:, None])
    )
    rank = jnp.sum(ahead.astype(jnp.int32), axis=1)
    chosen = rank[None, :] == block_ids[:, None]
    slot = jnp.sum(
        jnp.where(block_shuffle[0][:, None] == block_ids[None, :], block_ids[:, None], 0), axis=0
    )
    batch = slot // (blocks // devices)
    order = jnp.sum(jnp.where(chosen, block_ids[None, :], 0), axis=1)
    counts = jnp.sum(jnp.where(chosen, section_counts[None, :], 0), axis=1)
    batches = jnp.sum(jnp.where(chosen, batch[None, :], 0), axis=1)
    rates = pack_rates(rate_exponents, rows, steps)
    net = pack_net(inverses, stoichiometry, rows, steps)
    out = react(order, counts, batches, place, own, near, far, comp, mixing_rate, cell_index, rates, net)
    return jnp.transpose(out, (1, 0, 2))


def solution(mesh):
    both = ("gx", "yz")
    in_specs = (
        P(both, None, None),
        P(both, None),
        P(both, None),
        P(both, None),
        P(both),
        P(both, None),
        P(both, None, None),
        P(),
        P(),
    )
    return jax.shard_map(
        local, mesh=mesh, in_specs=in_specs, out_specs=P(both, None, None), check_vma=False
    )
```

```python
import functools

import jax
import jax.numpy as jnp
from jax import lax
from jax.experimental import pallas as pl
from jax.experimental.pallas import tpu as pltpu
from jax.sharding import PartitionSpec as P


STEP = 0.25
CELL_DEV = 128
SMAX = 6
LOW = 256
BF16 = jnp.bfloat16
F32 = jnp.float32


def round_up(value, multiple):
    return -(-value // multiple) * multiple


def moments_kernel(place_ref, comp_ref, mass_ref, cell_ref, out_ref, acc_ref, *, high, rows):
    step = pl.program_id(0)
    species, step_blocks, lanes = comp_ref.shape
    flat = comp_ref.reshape(species * step_blocks, lanes)

    @pl.when(step == 0)
    def _():
        acc_ref[...] = jnp.zeros_like(acc_ref)

    iota_low = lax.broadcasted_iota(jnp.int32, (LOW, lanes), 0).astype(F32).astype(BF16)
    local = cell_ref[...] - place_ref[0]
    hi = (local // LOW).astype(F32)
    lo = (local % LOW).astype(F32)
    zeros = jnp.zeros((rows - species - 1, lanes), F32)
    tables, spreads = [], []
    for b in range(step_blocks):
        m = mass_ref[b : b + 1, :]
        w = flat[pl.ds(b, species, stride=step_blocks), :] * m
        v = jnp.concatenate([w, m, zeros], axis=0)
        upper = v.astype(BF16).astype(F32)
        pieces = jnp.concatenate([upper, v - upper], axis=0).astype(BF16)
        low_row = jnp.broadcast_to(lo[b : b + 1, :], (LOW, lanes)).astype(BF16)
        tables.append(jnp.where(low_row == iota_low, BF16(1), BF16(0)))
        high_row = jnp.broadcast_to(hi[b : b + 1, :], (2 * rows, lanes)).astype(BF16)
        spreads.append(
            jnp.concatenate(
                [jnp.where(high_row == BF16(h), pieces, BF16(0)) for h in range(high)], axis=0
            )
        )
    table = jnp.concatenate(tables, axis=1)
    spread = jnp.concatenate(spreads, axis=1)
    acc_ref[...] += lax.dot_general(
        spread, table, (((1,), (1,)), ((), ())), preferred_element_type=F32
    )

    @pl.when(step == pl.num_programs(0) - 1)
    def _():
        per = high // 3
        for h in range(high):
            top = h * 2 * rows
            total = acc_ref[top : top + rows, :] + acc_ref[top + rows : top + 2 * rows, :]
            slab = h // per
            slot = 0 if slab == 1 else place_ref[1 + slab // 2]
            out_ref[slot, :, (h % per) * LOW : (h % per + 1) * LOW] = total


def moments(place, comp, mass, cell, slab_cells, rows):
    species, blocks, lanes = comp.shape
    high = 3 * slab_cells // LOW
    step_blocks = min(32, blocks)
    return pl.pallas_call(
        functools.partial(moments_kernel, high=high, rows=rows),
        out_shape=jax.ShapeDtypeStruct((3, rows, slab_cells), F32),
        grid_spec=pltpu.PrefetchScalarGridSpec(
            num_scalar_prefetch=1,
            grid=(blocks // step_blocks,),
            in_specs=[
                pl.BlockSpec((species, step_blocks, lanes), lambda s, p: (0, s, 0)),
                pl.BlockSpec((step_blocks, lanes), lambda s, p: (s, 0)),
                pl.BlockSpec((step_blocks, lanes), lambda s, p: (s, 0)),
            ],
            out_specs=pl.BlockSpec((3, rows, slab_cells), lambda s, p: (0, 0, 0)),
            scratch_shapes=[pltpu.VMEM((2 * rows * high, LOW), F32)],
        ),
        compiler_params=pltpu.CompilerParams(vmem_limit_bytes=48 << 20),
        cost_estimate=pl.CostEstimate(
            flops=2 * blocks * lanes * high * LOW * 2 * rows, bytes_accessed=4 * comp.size, transcendentals=0
        ),
        name="moments",
    )(place, comp, mass, cell)


def react_kernel(
    length_ref, sched_ref, batch_ref, place_ref,
    own_ref, near_ref, far_ref, comp_ref, rate_ref, cell_ref, rates_ref, net_ref,
    out_ref, table_ref, state_ref, *, group, slots, chunk,
):
    species, blocks, lanes = comp_ref.shape
    rows, slab_cells = own_ref.shape
    flat = comp_ref.reshape(species * blocks, lanes)
    out_flat = out_ref.reshape(species * blocks, lanes)
    per = slab_cells // LOW
    high = 3 * per
    first = place_ref[0]
    left_near = place_ref[1] == 1
    spare = 2 * species - rows

    def widened(values):
        return jnp.concatenate([values, values[spare:species]], axis=0)

    for h in range(high):
        slab, cols = h // per, slice((h % per) * LOW, (h % per + 1) * LOW)
        if slab == 1:
            t = own_ref[:, cols]
        elif slab == 0:
            t = jnp.where(left_near, near_ref[:, cols], far_ref[:, cols])
        else:
            t = jnp.where(left_near, far_ref[:, cols], near_ref[:, cols])
        m = t[species : species + 1, :]
        mean = jnp.where(m > 0, widened(t[:species]) / m, 0.0)
        upper = mean.astype(BF16).astype(F32)
        table_ref[h * rows : (h + 1) * rows, :LOW] = upper
        table_ref[h * rows : (h + 1) * rows, LOW:] = mean - upper

    iota_low = lax.broadcasted_iota(jnp.int32, (LOW, lanes), 0).astype(F32).astype(BF16)

    def mix_group(g, carry):
        base = g * group
        hots, his = [], []
        for j in range(group):
            local = cell_ref[pl.ds(base + j, 1), :] - first
            low_row = jnp.broadcast_to((local % LOW).astype(F32), (LOW, lanes)).astype(BF16)
            his.append(local // LOW)
            hots.append(jnp.where(low_row == iota_low, BF16(1), BF16(0)))
        hot = jnp.concatenate(hots, axis=1)
        hot = jnp.concatenate([hot, hot], axis=0)
        picked = jnp.dot(table_ref[...].astype(BF16), hot, preferred_element_type=F32)
        for j in range(group):
            part = slice(j * lanes, (j + 1) * lanes)
            high_row = jnp.broadcast_to(his[j], (rows, lanes))
            looked = jnp.where(high_row == 0, picked[0:rows, part], 0.0)
            for h in range(1, high):
                looked = jnp.where(high_row == h, picked[h * rows : (h + 1) * rows, part], looked)
            decay = jnp.exp(-rate_ref[pl.ds(base + j, 1), :])
            c = widened(flat[pl.ds(base + j, species, stride=blocks), :])
            state_ref[base + j] = looked + (c - looked) * decay
        return carry

    lax.fori_loop(0, blocks // group, mix_group, 0)
    state_ref[blocks] = jnp.zeros((rows, lanes), F32)
    length = length_ref[0]

    def section(s, carry):
        ids = [sched_ref[j * length + s] for j in range(slots)]
        held = []
        for c in range(0, slots, chunk):
            x = jnp.concatenate([state_ref[ids[c + j]] for j in range(chunk)], axis=1)
            upper = x.astype(BF16).astype(F32)
            k1 = jnp.concatenate([upper, x - upper, upper[: 64 - 2 * rows]], axis=0).astype(BF16)
            t = jnp.tanh(jnp.dot(rates_ref[...], k1, preferred_element_type=F32))
            t_upper = t.astype(BF16).astype(F32)
            held.append((x, jnp.concatenate([t_upper, t - t_upper], axis=0).astype(BF16)))
        for c in range(0, slots, chunk):
            x, k2 = held[c // chunk]
            for p in range(0, chunk, 2):
                pair = (ids[c + p], ids[c + p + 1])
                net = jnp.concatenate([net_ref[batch_ref[i]] for i in pair], axis=0)
                f = jnp.dot(net, k2[:, p * lanes : (p + 2) * lanes], preferred_element_type=F32)
                for i in range(2):
                    cols = slice(i * lanes, (i + 1) * lanes)
                    top = 2 * i * rows
                    change = f[top : top + rows, cols] + f[top + rows : top + 2 * rows, cols]
                    state_ref[pair[i]] = x[:, (p + i) * lanes : (p + i + 1) * lanes] + STEP * change
        return carry

    lax.fori_loop(0, length, section, 0)

    def put_out(g, carry):
        for j in range(group):
            out_flat[pl.ds(g * group + j, species, stride=blocks), :] = state_ref[g * group + j, :species, :]
        return carry

    lax.fori_loop(0, blocks // group, put_out, 0)


def react(length, sched, batch, place, own, near, far, comp, rate, cell, rates, net, slots):
    species, blocks, lanes = comp.shape
    rows, slab_cells = own.shape
    high = 3 * slab_cells // LOW
    vmem = pl.BlockSpec(memory_space=pltpu.VMEM)
    return pl.pallas_call(
        functools.partial(react_kernel, group=min(16, blocks), slots=slots, chunk=8),
        out_shape=jax.ShapeDtypeStruct(comp.shape, F32),
        grid_spec=pltpu.PrefetchScalarGridSpec(
            num_scalar_prefetch=4,
            grid=(),
            in_specs=[vmem] * 8,
            out_specs=vmem,
            scratch_shapes=[
                pltpu.VMEM((rows * high, 2 * LOW), F32),
                pltpu.VMEM((blocks + 1, rows, lanes), F32),
            ],
        ),
        compiler_params=pltpu.CompilerParams(vmem_limit_bytes=56 << 20),
        cost_estimate=pl.CostEstimate(
            flops=2 * blocks * lanes * high * LOW * 2 * rows, bytes_accessed=8 * comp.size, transcendentals=0
        ),
        name="react",
    )(length, sched, batch, place, own, near, far, comp, rate, cell, rates, net)


def split_two(values):
    upper = lax.reduce_precision(values, 8, 7)
    return upper, lax.reduce_precision(values - upper, 8, 7)


def pack_rates(rates, rows, steps):
    reactions, species = rates.shape
    spare = 2 * species - rows
    upper, lower = split_two(jnp.pad(rates, ((0, steps - reactions), (0, 0))))
    zeros = jnp.zeros((steps, rows - species), F32)
    return jnp.concatenate([upper, lower[:, spare:], upper, zeros, lower[:, :spare]], axis=1).astype(BF16)


def pack_net(inverse, stoichiometry, rows, steps):
    species = inverse.shape[1]
    reactions = stoichiometry.shape[1]
    inverse = jnp.concatenate([inverse, inverse[:, 2 * species - rows :]], axis=1)
    stoichiometry = jnp.pad(stoichiometry, ((0, 0), (0, steps - reactions)))
    net = jnp.einsum("qij,jr->qir", inverse, stoichiometry, precision=lax.Precision.HIGHEST)
    upper, lower = split_two(net)
    return jnp.concatenate(
        [jnp.concatenate([upper, upper], axis=2), jnp.concatenate([lower, jnp.zeros_like(lower)], axis=2)],
        axis=1,
    ).astype(BF16)


def section_schedule(counts, slots):
    blocks = counts.shape[0]
    ids = jnp.arange(blocks, dtype=jnp.int32)
    ends = jnp.sum(jnp.where(ids[None, :] <= ids[:, None], counts[None, :], 0), axis=1)
    total = jnp.sum(counts)
    length = jnp.maximum(jnp.max(counts), (total + slots - 1) // slots)
    places = jnp.arange(round_up(SMAX * blocks + slots, 128), dtype=jnp.int32)
    sched = jnp.sum((ends[:, None] <= places[None, :]).astype(jnp.int32), axis=0)
    return length.reshape(1).astype(jnp.int32), sched


def flat_inverse(inverse):
    size = inverse.shape[0] * inverse.shape[1]
    return jnp.pad(inverse.reshape(size), (0, round_up(size, 128) - size)).reshape(1, -1, 128)


def join(values, axis, distance):
    count = lax.axis_size(axis)
    got = lax.ppermute(values, axis, [(i, i ^ distance) for i in range(count)])
    return jnp.concatenate([values, got], axis=0)


def swap_pairs(near, far):
    count = lax.axis_size("gx")
    first = [(i, i ^ 1) for i in range(count) if i ^ 1 < count]
    second = [(i, i - 1 if i % 2 == 0 else i + 1) for i in range(count)]
    second = [(i, j) for i, j in second if 0 <= j < count]
    return lax.ppermute(near, "gx", first), lax.ppermute(far, "gx", second)


def local(
    composition, particle_mass, mixing_rate, cell_index, section_counts, block_shuffle,
    batch_inverse, rate_exponents, stoichiometry,
):
    blocks, species, lanes = composition.shape
    reactions = rate_exponents.shape[0]
    slabs, columns = lax.axis_size("gx"), lax.axis_size("yz")
    devices = slabs * columns
    slab_cells = CELL_DEV * columns
    rows = round_up(species + 1, 8)
    steps = round_up(reactions, 8)
    slab, column = lax.axis_index("gx"), lax.axis_index("yz")
    odd = slab % 2
    place = jnp.stack([(slab - 1) * slab_cells, 2 - odd, 1 + odd]).astype(jnp.int32)

    hops = [("yz", d) for d in (1 << k for k in range((columns - 1).bit_length()))]
    hops += [("gx", d) for d in (1 << k for k in range((slabs - 1).bit_length()))]
    inverses = flat_inverse(batch_inverse[0])
    comp = jnp.transpose(composition, (1, 0, 2))
    partial = moments(place, comp, particle_mass, cell_index, slab_cells, rows)
    near, far = partial[1], partial[2]
    (near, far, inverses) = lax.optimization_barrier((near, far, inverses))
    got_near, got_far = swap_pairs(near, far)
    inverses = join(inverses, *hops[0])
    own = partial[0] + got_near + got_far
    at = 1
    distance = 1
    while distance < columns:
        own, inverses = lax.optimization_barrier((own, inverses))
        own = own + lax.ppermute(own, "yz", [(i, i ^ distance) for i in range(columns)])
        if at < len(hops):
            inverses = join(inverses, *hops[at])
        at += 1
        distance *= 2
    while at < len(hops):
        inverses = join(inverses, *hops[at])
        at += 1
    near, far = swap_pairs(own, own)

    block_ids = jnp.arange(blocks, dtype=jnp.int32)
    slots = min(32, blocks)
    length, sched = section_schedule(section_counts, slots)
    slot = jnp.sum(
        jnp.where(block_shuffle[0][:, None] == block_ids[None, :], block_ids[:, None], 0), axis=0
    )
    batch = (slot // (blocks // devices)) ^ (slab * columns + column)
    batch = jnp.pad(batch, (0, 128))
    size = species * species
    matrices = inverses.reshape(devices, -1)[:, :size].reshape(devices, species, species)
    rates = pack_rates(rate_exponents, rows, steps)
    net = pack_net(matrices, stoichiometry, rows, steps)
    out = react(
        length, sched, batch, place, own, near, far, comp, mixing_rate, cell_index, rates, net, slots
    )
    return jnp.transpose(out, (1, 0, 2))


def solution(mesh):
    both = ("gx", "yz")
    in_specs = (
        P(both, None, None),
        P(both, None),
        P(both, None),
        P(both, None),
        P(both),
        P(both, None),
        P(both, None, None),
        P(),
        P(),
    )
    return jax.shard_map(
        local, mesh=mesh, in_specs=in_specs, out_specs=P(both, None, None), check_vma=False
    )
```

```python
import functools

import jax
import jax.numpy as jnp
from jax import lax
from jax.experimental import pallas as pl
from jax.experimental.pallas import tpu as pltpu
from jax.sharding import PartitionSpec as P


STEP = 0.25
CELL_DEV = 128
SMAX = 6
LOW = 256
BF16 = jnp.bfloat16
F32 = jnp.float32


def round_up(value, multiple):
    return -(-value // multiple) * multiple


def moments_kernel(place_ref, comp_ref, mass_ref, cell_ref, out_ref, acc_ref, *, high, rows):
    step = pl.program_id(0)
    species, step_blocks, lanes = comp_ref.shape
    flat = comp_ref.reshape(species * step_blocks, lanes)

    @pl.when(step == 0)
    def _():
        acc_ref[...] = jnp.zeros_like(acc_ref)

    iota_low = lax.broadcasted_iota(jnp.int32, (LOW, lanes), 0).astype(F32).astype(BF16)
    local = cell_ref[...] - place_ref[0]
    hi = (local // LOW).astype(F32)
    lo = (local % LOW).astype(F32)
    zeros = jnp.zeros((rows - species - 1, lanes), F32)
    tables, spreads = [], []
    for b in range(step_blocks):
        m = mass_ref[b : b + 1, :]
        w = flat[pl.ds(b, species, stride=step_blocks), :] * m
        v = jnp.concatenate([w, m, zeros], axis=0)
        upper = v.astype(BF16).astype(F32)
        pieces = jnp.concatenate([upper, v - upper], axis=0).astype(BF16)
        low_row = jnp.broadcast_to(lo[b : b + 1, :], (LOW, lanes)).astype(BF16)
        tables.append(jnp.where(low_row == iota_low, BF16(1), BF16(0)))
        high_row = jnp.broadcast_to(hi[b : b + 1, :], (2 * rows, lanes)).astype(BF16)
        spreads.append(
            jnp.concatenate(
                [jnp.where(high_row == BF16(h), pieces, BF16(0)) for h in range(high)], axis=0
            )
        )
    table = jnp.concatenate(tables, axis=1)
    spread = jnp.concatenate(spreads, axis=1)
    acc_ref[...] += lax.dot_general(
        spread, table, (((1,), (1,)), ((), ())), preferred_element_type=F32
    )

    @pl.when(step == pl.num_programs(0) - 1)
    def _():
        per = high // 3
        width = per * LOW // lanes
        kept = species + 1
        out_flat = out_ref.reshape(3 * kept * width, lanes)
        for h in range(high):
            top = h * 2 * rows
            slab = h // per
            slot = 0 if slab == 1 else place_ref[1 + slab // 2]
            for c in range(LOW // lanes):
                cols = slice(c * lanes, (c + 1) * lanes)
                total = acc_ref[top : top + rows, cols] + acc_ref[top + rows : top + 2 * rows, cols]
                start = slot * kept * width + (h % per) * (LOW // lanes) + c
                out_flat[pl.ds(start, kept, stride=width), :] = total[:kept]


def moments(place, comp, mass, cell, slab_cells, rows):
    species, blocks, lanes = comp.shape
    high = 3 * slab_cells // LOW
    step_blocks = min(32, blocks)
    sums = (species + 1) * slab_cells // lanes
    return pl.pallas_call(
        functools.partial(moments_kernel, high=high, rows=rows),
        out_shape=jax.ShapeDtypeStruct((3, sums, lanes), F32),
        grid_spec=pltpu.PrefetchScalarGridSpec(
            num_scalar_prefetch=1,
            grid=(blocks // step_blocks,),
            in_specs=[
                pl.BlockSpec((species, step_blocks, lanes), lambda s, p: (0, s, 0)),
                pl.BlockSpec((step_blocks, lanes), lambda s, p: (s, 0)),
                pl.BlockSpec((step_blocks, lanes), lambda s, p: (s, 0)),
            ],
            out_specs=pl.BlockSpec((3, sums, lanes), lambda s, p: (0, 0, 0)),
            scratch_shapes=[pltpu.VMEM((2 * rows * high, LOW), F32)],
        ),
        compiler_params=pltpu.CompilerParams(vmem_limit_bytes=48 << 20),
        cost_estimate=pl.CostEstimate(
            flops=2 * blocks * lanes * high * LOW * 2 * rows, bytes_accessed=4 * comp.size, transcendentals=0
        ),
        name="moments",
    )(place, comp, mass, cell)


def react_kernel(
    length_ref, sched_ref, batch_ref, place_ref,
    own_ref, near_ref, far_ref, comp_ref, rate_ref, cell_ref, rates_ref, net_ref,
    out_ref, table_ref, state_ref, *, group, slots, chunk,
):
    species, blocks, lanes = comp_ref.shape
    width = own_ref.shape[0] // (species + 1)
    rows = state_ref.shape[1]
    flat = comp_ref.reshape(species * blocks, lanes)
    out_flat = out_ref.reshape(species * blocks, lanes)
    parts = LOW // lanes
    per = width // parts
    high = 3 * per
    first = place_ref[0]
    left_near = place_ref[1] == 1
    spare = 2 * species - rows

    def widened(values):
        return jnp.concatenate([values, values[spare:species]], axis=0)

    for h in range(high):
        slab = h // per

        def cells(ref):
            start = (h % per) * parts
            return jnp.concatenate(
                [ref[pl.ds(start + c, species + 1, stride=width), :] for c in range(parts)], axis=1
            )

        if slab == 1:
            t = cells(own_ref)
        elif slab == 0:
            t = jnp.where(left_near, cells(near_ref), cells(far_ref))
        else:
            t = jnp.where(left_near, cells(far_ref), cells(near_ref))
        m = t[species : species + 1, :]
        mean = jnp.where(m > 0, widened(t[:species]) / m, 0.0)
        upper = mean.astype(BF16).astype(F32)
        table_ref[h * rows : (h + 1) * rows, :LOW] = upper
        table_ref[h * rows : (h + 1) * rows, LOW:] = mean - upper

    iota_low = lax.broadcasted_iota(jnp.int32, (LOW, lanes), 0).astype(F32).astype(BF16)

    def mix_group(g, carry):
        base = g * group
        hots, his = [], []
        for j in range(group):
            local = cell_ref[pl.ds(base + j, 1), :] - first
            low_row = jnp.broadcast_to((local % LOW).astype(F32), (LOW, lanes)).astype(BF16)
            his.append(local // LOW)
            hots.append(jnp.where(low_row == iota_low, BF16(1), BF16(0)))
        hot = jnp.concatenate(hots, axis=1)
        hot = jnp.concatenate([hot, hot], axis=0)
        picked = jnp.dot(table_ref[...].astype(BF16), hot, preferred_element_type=F32)
        for j in range(group):
            part = slice(j * lanes, (j + 1) * lanes)
            high_row = jnp.broadcast_to(his[j], (rows, lanes))
            looked = jnp.where(high_row == 0, picked[0:rows, part], 0.0)
            for h in range(1, high):
                looked = jnp.where(high_row == h, picked[h * rows : (h + 1) * rows, part], looked)
            decay = jnp.exp(-rate_ref[pl.ds(base + j, 1), :])
            c = widened(flat[pl.ds(base + j, species, stride=blocks), :])
            state_ref[base + j] = looked + (c - looked) * decay
        return carry

    lax.fori_loop(0, blocks // group, mix_group, 0)
    state_ref[blocks] = jnp.zeros((rows, lanes), F32)
    length = length_ref[0]

    def section(s, carry):
        ids = [sched_ref[j * length + s] for j in range(slots)]
        held = []
        for c in range(0, slots, chunk):
            x = jnp.concatenate([state_ref[ids[c + j]] for j in range(chunk)], axis=1)
            upper = x.astype(BF16).astype(F32)
            k1 = jnp.concatenate([upper, x - upper, upper[: 64 - 2 * rows]], axis=0).astype(BF16)
            t = jnp.tanh(jnp.dot(rates_ref[...], k1, preferred_element_type=F32))
            t_upper = t.astype(BF16).astype(F32)
            held.append((x, jnp.concatenate([t_upper, t - t_upper], axis=0).astype(BF16)))
        for c in range(0, slots, chunk):
            x, k2 = held[c // chunk]
            for p in range(0, chunk, 2):
                pair = (ids[c + p], ids[c + p + 1])
                net = jnp.concatenate([net_ref[batch_ref[i]] for i in pair], axis=0)
                f = jnp.dot(net, k2[:, p * lanes : (p + 2) * lanes], preferred_element_type=F32)
                for i in range(2):
                    cols = slice(i * lanes, (i + 1) * lanes)
                    top = 2 * i * rows
                    change = f[top : top + rows, cols] + f[top + rows : top + 2 * rows, cols]
                    state_ref[pair[i]] = x[:, (p + i) * lanes : (p + i + 1) * lanes] + STEP * change
        return carry

    lax.fori_loop(0, length, section, 0)

    def put_out(g, carry):
        for j in range(group):
            out_flat[pl.ds(g * group + j, species, stride=blocks), :] = state_ref[g * group + j, :species, :]
        return carry

    lax.fori_loop(0, blocks // group, put_out, 0)


def react(length, sched, batch, place, own, near, far, comp, rate, cell, rates, net, slots):
    species, blocks, lanes = comp.shape
    rows = round_up(species + 1, 8)
    high = 3 * (own.shape[0] * lanes // (species + 1)) // LOW
    vmem = pl.BlockSpec(memory_space=pltpu.VMEM)
    return pl.pallas_call(
        functools.partial(react_kernel, group=min(16, blocks), slots=slots, chunk=8),
        out_shape=jax.ShapeDtypeStruct(comp.shape, F32),
        grid_spec=pltpu.PrefetchScalarGridSpec(
            num_scalar_prefetch=4,
            grid=(),
            in_specs=[vmem] * 8,
            out_specs=vmem,
            scratch_shapes=[
                pltpu.VMEM((rows * high, 2 * LOW), F32),
                pltpu.VMEM((blocks + 1, rows, lanes), F32),
            ],
        ),
        compiler_params=pltpu.CompilerParams(vmem_limit_bytes=28 << 20),
        cost_estimate=pl.CostEstimate(
            flops=2 * blocks * lanes * high * LOW * 2 * rows, bytes_accessed=8 * comp.size, transcendentals=0
        ),
        name="react",
    )(length, sched, batch, place, own, near, far, comp, rate, cell, rates, net)


def split_two(values):
    upper = lax.reduce_precision(values, 8, 7)
    return upper, lax.reduce_precision(values - upper, 8, 7)


def pack_rates(rates, rows, steps):
    reactions, species = rates.shape
    spare = 2 * species - rows
    upper, lower = split_two(jnp.pad(rates, ((0, steps - reactions), (0, 0))))
    zeros = jnp.zeros((steps, rows - species), F32)
    return jnp.concatenate([upper, lower[:, spare:], upper, zeros, lower[:, :spare]], axis=1).astype(BF16)


def pack_net(inverse, stoichiometry, rows, steps):
    species = inverse.shape[1]
    reactions = stoichiometry.shape[1]
    inverse = jnp.concatenate([inverse, inverse[:, 2 * species - rows :]], axis=1)
    stoichiometry = jnp.pad(stoichiometry, ((0, 0), (0, steps - reactions)))
    net = jnp.einsum("qij,jr->qir", inverse, stoichiometry, precision=lax.Precision.HIGHEST)
    upper, lower = split_two(net)
    return jnp.concatenate(
        [jnp.concatenate([upper, upper], axis=2), jnp.concatenate([lower, jnp.zeros_like(lower)], axis=2)],
        axis=1,
    ).astype(BF16)


def section_schedule(counts, slots):
    blocks = counts.shape[0]
    ids = jnp.arange(blocks, dtype=jnp.int32)
    ends = jnp.sum(jnp.where(ids[None, :] <= ids[:, None], counts[None, :], 0), axis=1)
    total = jnp.sum(counts)
    length = jnp.maximum(jnp.max(counts), (total + slots - 1) // slots)
    places = jnp.arange(round_up(SMAX * blocks + slots, 128), dtype=jnp.int32)
    sched = jnp.sum((ends[:, None] <= places[None, :]).astype(jnp.int32), axis=0)
    return length.reshape(1).astype(jnp.int32), sched


def flat_inverse(inverse, lanes):
    size = inverse.shape[0] * inverse.shape[1]
    return jnp.pad(inverse.reshape(size), (0, round_up(size, lanes) - size)).reshape(-1, lanes)


def from_partner(values, axis, distance):
    count = lax.axis_size(axis)
    return lax.ppermute(values, axis, [(i, i ^ distance) for i in range(count)])


def swap_pairs(near, far):
    count = lax.axis_size("gx")
    first = [(i, i ^ 1) for i in range(count) if i ^ 1 < count]
    second = [(i, i - 1 if i % 2 == 0 else i + 1) for i in range(count)]
    second = [(i, j) for i, j in second if 0 <= j < count]
    return lax.ppermute(near, "gx", first), lax.ppermute(far, "gx", second)


def local(
    composition, particle_mass, mixing_rate, cell_index, section_counts, block_shuffle,
    batch_inverse, rate_exponents, stoichiometry,
):
    blocks, species, lanes = composition.shape
    reactions = rate_exponents.shape[0]
    slabs, columns = lax.axis_size("gx"), lax.axis_size("yz")
    devices = slabs * columns
    slab_cells = CELL_DEV * columns
    rows = round_up(species + 1, 8)
    steps = round_up(reactions, 8)
    slab, column = lax.axis_index("gx"), lax.axis_index("yz")
    odd = slab % 2
    place = jnp.stack([(slab - 1) * slab_cells, 2 - odd, 1 + odd]).astype(jnp.int32)

    inverses = flat_inverse(batch_inverse[0], lanes)
    inverses = jnp.concatenate([inverses, from_partner(inverses, "gx", 1)], axis=0)
    comp = jnp.transpose(composition, (1, 0, 2))
    held = [pltpu.with_memory_space_constraint(v, pltpu.HBM) for v in (comp, particle_mass, cell_index)]
    partial = moments(place, *held, slab_cells, rows)
    near, far = partial[1], partial[2]
    got_near, got_far = swap_pairs(near, far)
    distance = 2
    while distance < slabs:
        near, far, inverses = lax.optimization_barrier((near, far, inverses))
        inverses = jnp.concatenate([inverses, from_partner(inverses, "gx", distance)], axis=0)
        distance *= 2
    own = partial[0] + got_near + got_far
    sums = own.shape[0]
    distance = 1
    while distance < columns:
        got = from_partner(jnp.concatenate([own, inverses], axis=0), "yz", distance)
        own = own + got[:sums]
        inverses = jnp.concatenate([inverses, got[sums:]], axis=0)
        distance *= 2
    near, far = swap_pairs(own, own)

    block_ids = jnp.arange(blocks, dtype=jnp.int32)
    slots = min(32, blocks)
    length, sched = section_schedule(section_counts, slots)
    slot = jnp.sum(
        jnp.where(block_shuffle[0][:, None] == block_ids[None, :], block_ids[:, None], 0), axis=0
    )
    batch = (slot // (blocks // devices)) ^ (slab * columns + column)
    batch = batch % columns * slabs + batch // columns
    batch = jnp.pad(batch, (0, 128))
    size = species * species
    matrices = inverses.reshape(devices, -1)[:, :size].reshape(devices, species, species)
    rates = pack_rates(rate_exponents, rows, steps)
    net = pack_net(matrices, stoichiometry, rows, steps)
    out = react(
        length, sched, batch, place, own, near, far, comp, mixing_rate, cell_index, rates, net, slots
    )
    return jnp.transpose(out, (1, 0, 2))


def solution(mesh):
    both = ("gx", "yz")
    in_specs = (
        P(both, None, None),
        P(both, None),
        P(both, None),
        P(both, None),
        P(both),
        P(both, None),
        P(both, None, None),
        P(),
        P(),
    )
    return jax.shard_map(
        local, mesh=mesh, in_specs=in_specs, out_specs=P(both, None, None), check_vma=False
    )
```

```python
import functools

import jax
import jax.numpy as jnp
from jax import lax
from jax.experimental import pallas as pl
from jax.experimental.pallas import tpu as pltpu
from jax.sharding import PartitionSpec as P


STEP = 0.25
CELL_DEV = 128
SMAX = 6
LOW = 256
BF16 = jnp.bfloat16
F32 = jnp.float32


def round_up(value, multiple):
    return -(-value // multiple) * multiple


def split_in_two(values):
    upper = values.astype(BF16).astype(F32)
    return upper, values - upper


def moments_kernel(place_ref, comp_ref, mass_ref, cell_ref, out_ref, acc_ref, *, high, rows):
    step = pl.program_id(0)
    species, step_blocks, lanes = comp_ref.shape
    flat = comp_ref.reshape(species * step_blocks, lanes)

    @pl.when(step == 0)
    def _():
        acc_ref[...] = jnp.zeros_like(acc_ref)

    iota_low = lax.broadcasted_iota(jnp.int32, (LOW, lanes), 0).astype(F32).astype(BF16)
    local = cell_ref[...] - place_ref[0]
    hi = (local // LOW).astype(F32)
    lo = (local % LOW).astype(F32)
    zeros = jnp.zeros((rows - species - 1, lanes), F32)
    tables, spreads = [], []
    for b in range(step_blocks):
        m = mass_ref[b : b + 1, :]
        w = flat[pl.ds(b, species, stride=step_blocks), :] * m
        v = jnp.concatenate([w, m, zeros], axis=0)
        upper = v.astype(BF16).astype(F32)
        pieces = jnp.concatenate([upper, v - upper], axis=0).astype(BF16)
        low_row = jnp.broadcast_to(lo[b : b + 1, :], (LOW, lanes)).astype(BF16)
        tables.append(jnp.where(low_row == iota_low, BF16(1), BF16(0)))
        high_row = jnp.broadcast_to(hi[b : b + 1, :], (2 * rows, lanes)).astype(BF16)
        spreads.append(
            jnp.concatenate(
                [jnp.where(high_row == BF16(h), pieces, BF16(0)) for h in range(high)], axis=0
            )
        )
    table = jnp.concatenate(tables, axis=1)
    spread = jnp.concatenate(spreads, axis=1)
    acc_ref[...] += lax.dot_general(
        spread, table, (((1,), (1,)), ((), ())), preferred_element_type=F32
    )

    @pl.when(step == pl.num_programs(0) - 1)
    def _():
        per = high // 3
        width = per * LOW // lanes
        kept = species + 1
        out_flat = out_ref.reshape(3 * kept * width, lanes)
        for h in range(high):
            top = h * 2 * rows
            slab = h // per
            slot = 0 if slab == 1 else place_ref[1 + slab // 2]
            for c in range(LOW // lanes):
                cols = slice(c * lanes, (c + 1) * lanes)
                total = acc_ref[top : top + rows, cols] + acc_ref[top + rows : top + 2 * rows, cols]
                start = slot * kept * width + (h % per) * (LOW // lanes) + c
                out_flat[pl.ds(start, kept, stride=width), :] = total[:kept]


def moments(place, comp, mass, cell, slab_cells, rows):
    species, blocks, lanes = comp.shape
    high = 3 * slab_cells // LOW
    step_blocks = min(32, blocks)
    sums = (species + 1) * slab_cells // lanes
    return pl.pallas_call(
        functools.partial(moments_kernel, high=high, rows=rows),
        out_shape=jax.ShapeDtypeStruct((3, sums, lanes), F32),
        grid_spec=pltpu.PrefetchScalarGridSpec(
            num_scalar_prefetch=1,
            grid=(blocks // step_blocks,),
            in_specs=[
                pl.BlockSpec((species, step_blocks, lanes), lambda s, p: (0, s, 0)),
                pl.BlockSpec((step_blocks, lanes), lambda s, p: (s, 0)),
                pl.BlockSpec((step_blocks, lanes), lambda s, p: (s, 0)),
            ],
            out_specs=pl.BlockSpec((3, sums, lanes), lambda s, p: (0, 0, 0)),
            scratch_shapes=[pltpu.VMEM((2 * rows * high, LOW), F32)],
        ),
        compiler_params=pltpu.CompilerParams(vmem_limit_bytes=48 << 20),
        cost_estimate=pl.CostEstimate(
            flops=2 * blocks * lanes * high * LOW * 2 * rows, bytes_accessed=4 * comp.size, transcendentals=0
        ),
        name="moments",
    )(place, comp, mass, cell)


def react_kernel(
    length_ref, sched_ref, batch_ref, place_ref,
    own_ref, near_ref, far_ref, comp_ref, rate_ref, cell_ref, rates_ref, net_ref,
    out_ref, table_ref, state_ref, *, group, slots, chunk,
):
    species, blocks, lanes = comp_ref.shape
    width = own_ref.shape[0] // (species + 1)
    rows = state_ref.shape[1]
    flat = comp_ref.reshape(species * blocks, lanes)
    out_flat = out_ref.reshape(species * blocks, lanes)
    parts = LOW // lanes
    per = width // parts
    high = 3 * per
    first = place_ref[0]
    left_near = place_ref[1] == 1
    half = rows - species

    for h in range(high):
        slab = h // per

        def cells(ref):
            start = (h % per) * parts
            return jnp.concatenate(
                [ref[pl.ds(start + c, species + 1, stride=width), :] for c in range(parts)], axis=1
            )

        if slab == 1:
            t = cells(own_ref)
        elif slab == 0:
            t = jnp.where(left_near, cells(near_ref), cells(far_ref))
        else:
            t = jnp.where(left_near, cells(far_ref), cells(near_ref))
        m = t[species : species + 1, :]
        mean = jnp.where(m > 0, t[:species] / m, 0.0)
        for side, piece in enumerate(split_in_two(mean)):
            cols = slice(side * LOW, (side + 1) * LOW)
            table_ref[h * 16 : h * 16 + 16, cols] = piece[:16]
            rest_top = 16 * high + half * h
            table_ref[rest_top : rest_top + half, cols] = piece[16:]

    iota_low = lax.broadcasted_iota(jnp.int32, (LOW, lanes), 0).astype(F32).astype(BF16)

    second = lax.broadcasted_iota(jnp.int32, (2 * half, lanes), 0) // half

    def mix_group(g, carry):
        base = g * group
        hots, his = [], []
        for j in range(group):
            local = cell_ref[pl.ds(base + j, 1), :] - first
            low_row = jnp.broadcast_to((local % LOW).astype(F32), (LOW, lanes)).astype(BF16)
            his.append(local // LOW)
            hots.append(jnp.where(low_row == iota_low, BF16(1), BF16(0)))
        hot = jnp.concatenate(hots, axis=1)
        hot = jnp.concatenate([hot, hot], axis=0)
        picked = jnp.dot(table_ref[...].astype(BF16), hot, preferred_element_type=F32)
        for j in range(group):
            part = slice(j * lanes, (j + 1) * lanes)
            high_row = jnp.broadcast_to(his[j], (16, lanes))
            high_half = jnp.broadcast_to(his[j], (2 * half, lanes)) - second
            looked = jnp.where(high_row == 0, picked[0:16, part], 0.0)
            for h in range(1, high):
                looked = jnp.where(high_row == h, picked[h * 16 : h * 16 + 16, part], looked)
            rest = jnp.zeros((2 * half, lanes), F32)
            for h in range(0, high, 2):
                top = 16 * high + half * h
                rest = jnp.where(high_half == h, picked[top : top + 2 * half, part], rest)
            rest = rest + pltpu.roll(rest, half, 0)
            looked = jnp.concatenate([looked, rest], axis=0)
            decay = jnp.exp(-rate_ref[pl.ds(base + j, 1), :])
            c = flat[pl.ds(base + j, species, stride=blocks), :]
            c = jnp.concatenate([c, c[16:]], axis=0)
            state_ref[base + j] = looked + (c - looked) * decay
        return carry

    lax.fori_loop(0, blocks // group, mix_group, 0)
    state_ref[blocks] = jnp.zeros((rows, lanes), F32)
    length = length_ref[0]

    def section(s, carry):
        ids = [sched_ref[j * length + s] for j in range(slots)]
        held = []
        for c in range(0, slots, chunk):
            x = jnp.concatenate([state_ref[ids[c + j]] for j in range(chunk)], axis=1)
            upper, lower = split_in_two(x)
            k1 = jnp.concatenate([upper, lower, upper[:16]], axis=0).astype(BF16)
            t = jnp.tanh(jnp.dot(rates_ref[...], k1, preferred_element_type=F32))
            held.append((x, jnp.concatenate(split_in_two(t), axis=0).astype(BF16)))
        for c in range(0, slots, chunk):
            x, k2 = held[c // chunk]
            for p in range(0, chunk, 2):
                pair = (ids[c + p], ids[c + p + 1])
                net = jnp.concatenate([net_ref[batch_ref[i]] for i in pair], axis=0)
                f = jnp.dot(net, k2[:, p * lanes : (p + 2) * lanes], preferred_element_type=F32)
                for i in range(2):
                    cols = slice(i * lanes, (i + 1) * lanes)
                    top = 2 * i * rows
                    change = f[top : top + rows, cols] + f[top + rows : top + 2 * rows, cols]
                    state_ref[pair[i]] = x[:, (p + i) * lanes : (p + i + 1) * lanes] + STEP * change
        return carry

    lax.fori_loop(0, length, section, 0)

    def put_out(g, carry):
        for j in range(group):
            out_flat[pl.ds(g * group + j, species, stride=blocks), :] = state_ref[g * group + j, :species, :]
        return carry

    lax.fori_loop(0, blocks // group, put_out, 0)


def react(length, sched, batch, place, own, near, far, comp, rate, cell, rates, net, slots):
    species, blocks, lanes = comp.shape
    rows = round_up(species + 1, 8)
    high = 3 * (own.shape[0] * lanes // (species + 1)) // LOW
    vmem = pl.BlockSpec(memory_space=pltpu.VMEM)
    return pl.pallas_call(
        functools.partial(react_kernel, group=min(16, blocks), slots=slots, chunk=8),
        out_shape=jax.ShapeDtypeStruct(comp.shape, F32),
        grid_spec=pltpu.PrefetchScalarGridSpec(
            num_scalar_prefetch=4,
            grid=(),
            in_specs=[vmem] * 8,
            out_specs=vmem,
            scratch_shapes=[
                pltpu.VMEM((species * high, 2 * LOW), F32),
                pltpu.VMEM((blocks + 1, rows, lanes), F32),
            ],
        ),
        compiler_params=pltpu.CompilerParams(vmem_limit_bytes=28 << 20),
        cost_estimate=pl.CostEstimate(
            flops=2 * blocks * lanes * high * LOW * 2 * rows, bytes_accessed=8 * comp.size, transcendentals=0
        ),
        name="react",
    )(length, sched, batch, place, own, near, far, comp, rate, cell, rates, net)


def split_two(values):
    upper = lax.reduce_precision(values, 8, 7)
    return upper, lax.reduce_precision(values - upper, 8, 7)


def pack_rates(rates, rows, steps):
    reactions, species = rates.shape
    spare = 2 * species - rows
    upper, lower = split_two(jnp.pad(rates, ((0, steps - reactions), (0, 0))))
    zeros = jnp.zeros((steps, rows - species), F32)
    return jnp.concatenate([upper, lower[:, spare:], upper, zeros, lower[:, :spare]], axis=1).astype(BF16)


def pack_net(inverse, stoichiometry, rows, steps):
    species = inverse.shape[1]
    reactions = stoichiometry.shape[1]
    inverse = jnp.concatenate([inverse, inverse[:, 2 * species - rows :]], axis=1)
    stoichiometry = jnp.pad(stoichiometry, ((0, 0), (0, steps - reactions)))
    net = jnp.einsum("qij,jr->qir", inverse, stoichiometry, precision=lax.Precision.HIGHEST)
    upper, lower = split_two(net)
    return jnp.concatenate(
        [jnp.concatenate([upper, upper], axis=2), jnp.concatenate([lower, jnp.zeros_like(lower)], axis=2)],
        axis=1,
    ).astype(BF16)


def section_schedule(counts, slots):
    blocks = counts.shape[0]
    ids = jnp.arange(blocks, dtype=jnp.int32)
    ends = jnp.sum(jnp.where(ids[None, :] <= ids[:, None], counts[None, :], 0), axis=1)
    total = jnp.sum(counts)
    length = jnp.maximum(jnp.max(counts), (total + slots - 1) // slots)
    places = jnp.arange(round_up(SMAX * blocks + slots, 128), dtype=jnp.int32)
    sched = jnp.sum((ends[:, None] <= places[None, :]).astype(jnp.int32), axis=0)
    return length.reshape(1).astype(jnp.int32), sched


def flat_inverses(inverses, lanes):
    count = inverses.shape[0]
    size = inverses.shape[1] * inverses.shape[2]
    flat = jnp.pad(inverses.reshape(count, size), ((0, 0), (0, round_up(size, lanes) - size)))
    return flat.reshape(-1, lanes)


def from_partner(values, axis, distance):
    count = lax.axis_size(axis)
    return lax.ppermute(values, axis, [(i, i ^ distance) for i in range(count)])


def swap_pairs(near, far):
    count = lax.axis_size("gx")
    first = [(i, i ^ 1) for i in range(count) if i ^ 1 < count]
    second = [(i, i - 1 if i % 2 == 0 else i + 1) for i in range(count)]
    second = [(i, j) for i, j in second if 0 <= j < count]
    return lax.ppermute(near, "gx", first), lax.ppermute(far, "gx", second)


def local(
    composition, particle_mass, mixing_rate, cell_index, section_counts, block_shuffle,
    batch_inverse, rate_exponents, stoichiometry,
):
    blocks, species, lanes = composition.shape
    reactions = rate_exponents.shape[0]
    slabs, columns = lax.axis_size("gx"), lax.axis_size("yz")
    devices = slabs * columns
    slab_cells = CELL_DEV * columns
    rows = round_up(species + 1, 8)
    steps = round_up(reactions, 8)
    slab, column = lax.axis_index("gx"), lax.axis_index("yz")
    odd = slab % 2
    place = jnp.stack([(slab - 1) * slab_cells, 2 - odd, 1 + odd]).astype(jnp.int32)

    inverses = [batch_inverse]
    for distance in range(1, slabs):
        inverses.append(from_partner(batch_inverse, "gx", distance))
    comp = jnp.transpose(composition, (1, 0, 2))
    held = [pltpu.with_memory_space_constraint(v, pltpu.HBM) for v in (comp, particle_mass, cell_index)]
    partial = moments(place, *held, slab_cells, rows)
    near, far = partial[1], partial[2]
    got_near, got_far = swap_pairs(near, far)
    inverses = flat_inverses(jnp.concatenate(inverses, axis=0), lanes)
    own = partial[0] + got_near + got_far
    sums = own.shape[0]
    distance = 1
    while distance < columns:
        got = from_partner(jnp.concatenate([own, inverses], axis=0), "yz", distance)
        own = own + got[:sums]
        inverses = jnp.concatenate([inverses, got[sums:]], axis=0)
        distance *= 2
    near, far = swap_pairs(own, own)

    block_ids = jnp.arange(blocks, dtype=jnp.int32)
    slots = min(32, blocks)
    length, sched = section_schedule(section_counts, slots)
    slot = jnp.sum(
        jnp.where(block_shuffle[0][:, None] == block_ids[None, :], block_ids[:, None], 0), axis=0
    )
    batch = (slot // (blocks // devices)) ^ (slab * columns + column)
    batch = batch % columns * slabs + batch // columns
    batch = jnp.pad(batch, (0, 128))
    size = species * species
    matrices = inverses.reshape(devices, -1)[:, :size].reshape(devices, species, species)
    rates = pack_rates(rate_exponents, rows, steps)
    net = pack_net(matrices, stoichiometry, rows, steps)
    out = react(
        length, sched, batch, place, own, near, far, comp, mixing_rate, cell_index, rates, net, slots
    )
    return jnp.transpose(out, (1, 0, 2))


def solution(mesh):
    both = ("gx", "yz")
    in_specs = (
        P(both, None, None),
        P(both, None),
        P(both, None),
        P(both, None),
        P(both),
        P(both, None),
        P(both, None, None),
        P(),
        P(),
    )
    return jax.shard_map(
        local, mesh=mesh, in_specs=in_specs, out_specs=P(both, None, None), check_vma=False
    )
```

```python
import functools

import jax
import jax.numpy as jnp
from jax import lax
from jax.experimental import pallas as pl
from jax.experimental.pallas import tpu as pltpu
from jax.sharding import PartitionSpec as P


STEP = 0.25
CELL_DEV = 128
SMAX = 6
LOW = 256
BF16 = jnp.bfloat16
F32 = jnp.float32


def round_up(value, multiple):
    return -(-value // multiple) * multiple


def split_in_two(values):
    upper = values.astype(BF16).astype(F32)
    return upper, values - upper


def moments_kernel(place_ref, comp_ref, mass_ref, cell_ref, out_ref, acc_ref, *, slabs, per, rows):
    step = pl.program_id(0)
    species, step_blocks, lanes = comp_ref.shape
    flat = comp_ref.reshape(species * step_blocks, lanes)
    highs = [slab * per + c for slab in slabs for c in range(per)]

    @pl.when(step == 0)
    def _():
        acc_ref[...] = jnp.zeros_like(acc_ref)

    iota_low = lax.broadcasted_iota(jnp.int32, (LOW, lanes), 0).astype(F32).astype(BF16)
    local = cell_ref[...] - place_ref[0]
    hi = (local // LOW).astype(F32)
    lo = (local % LOW).astype(F32)
    zeros = jnp.zeros((rows - species - 1, lanes), F32)
    tables, spreads = [], []
    for b in range(step_blocks):
        m = mass_ref[b : b + 1, :]
        w = flat[pl.ds(b, species, stride=step_blocks), :] * m
        v = jnp.concatenate([w, m, zeros], axis=0)
        upper = v.astype(BF16).astype(F32)
        pieces = jnp.concatenate([upper, v - upper], axis=0).astype(BF16)
        low_row = jnp.broadcast_to(lo[b : b + 1, :], (LOW, lanes)).astype(BF16)
        tables.append(jnp.where(low_row == iota_low, BF16(1), BF16(0)))
        high_row = jnp.broadcast_to(hi[b : b + 1, :], (2 * rows, lanes)).astype(BF16)
        spreads.append(
            jnp.concatenate(
                [jnp.where(high_row == BF16(h), pieces, BF16(0)) for h in highs], axis=0
            )
        )
    table = jnp.concatenate(tables, axis=1)
    spread = jnp.concatenate(spreads, axis=1)
    acc_ref[...] += lax.dot_general(
        spread, table, (((1,), (1,)), ((), ())), preferred_element_type=F32
    )

    @pl.when(step == pl.num_programs(0) - 1)
    def _():
        width = per * LOW // lanes
        kept = species + 1
        out_flat = out_ref.reshape(len(slabs) * kept * width, lanes)
        for at, h in enumerate(highs):
            top = at * 2 * rows
            slab = h // per
            slot = 0 if slab == 1 else place_ref[1 + slab // 2]
            for c in range(LOW // lanes):
                cols = slice(c * lanes, (c + 1) * lanes)
                total = acc_ref[top : top + rows, cols] + acc_ref[top + rows : top + 2 * rows, cols]
                start = slot * kept * width + (h % per) * (LOW // lanes) + c
                out_flat[pl.ds(start, kept, stride=width), :] = total[:kept]


def moments(place, comp, mass, cell, slab_cells, rows, slabs):
    species, blocks, lanes = comp.shape
    per = slab_cells // LOW
    high = len(slabs) * per
    step_blocks = min(32, blocks)
    sums = (species + 1) * slab_cells // lanes
    return pl.pallas_call(
        functools.partial(moments_kernel, slabs=slabs, per=per, rows=rows),
        out_shape=jax.ShapeDtypeStruct((len(slabs), sums, lanes), F32),
        grid_spec=pltpu.PrefetchScalarGridSpec(
            num_scalar_prefetch=1,
            grid=(blocks // step_blocks,),
            in_specs=[
                pl.BlockSpec((species, step_blocks, lanes), lambda s, p: (0, s, 0)),
                pl.BlockSpec((step_blocks, lanes), lambda s, p: (s, 0)),
                pl.BlockSpec((step_blocks, lanes), lambda s, p: (s, 0)),
            ],
            out_specs=pl.BlockSpec((len(slabs), sums, lanes), lambda s, p: (0, 0, 0)),
            scratch_shapes=[pltpu.VMEM((2 * rows * high, LOW), F32)],
        ),
        compiler_params=pltpu.CompilerParams(vmem_limit_bytes=48 << 20),
        cost_estimate=pl.CostEstimate(
            flops=2 * blocks * lanes * high * LOW * 2 * rows, bytes_accessed=4 * comp.size, transcendentals=0
        ),
        name="moments",
    )(place, comp, mass, cell)


def react_kernel(
    length_ref, sched_ref, batch_ref, place_ref,
    own_ref, near_ref, far_ref, comp_ref, rate_ref, cell_ref, rates_ref, net_ref,
    out_ref, table_ref, state_ref, *, group, slots, chunk,
):
    species, blocks, lanes = comp_ref.shape
    width = own_ref.shape[0] // (species + 1)
    rows = state_ref.shape[1]
    flat = comp_ref.reshape(species * blocks, lanes)
    out_flat = out_ref.reshape(species * blocks, lanes)
    parts = LOW // lanes
    per = width // parts
    high = 3 * per
    first = place_ref[0]
    left_near = place_ref[1] == 0
    half = rows - species

    for h in range(high):
        slab = h // per

        def cells(ref):
            start = (h % per) * parts
            return jnp.concatenate(
                [ref[pl.ds(start + c, species + 1, stride=width), :] for c in range(parts)], axis=1
            )

        if slab == 1:
            t = cells(own_ref)
        elif slab == 0:
            t = jnp.where(left_near, cells(near_ref), cells(far_ref))
        else:
            t = jnp.where(left_near, cells(far_ref), cells(near_ref))
        m = t[species : species + 1, :]
        mean = jnp.where(m > 0, t[:species] / m, 0.0)
        for side, piece in enumerate(split_in_two(mean)):
            cols = slice(side * LOW, (side + 1) * LOW)
            table_ref[h * 16 : h * 16 + 16, cols] = piece[:16]
            rest_top = 16 * high + half * h
            table_ref[rest_top : rest_top + half, cols] = piece[16:]

    iota_low = lax.broadcasted_iota(jnp.int32, (LOW, lanes), 0).astype(F32).astype(BF16)

    second = lax.broadcasted_iota(jnp.int32, (2 * half, lanes), 0) // half

    def mix_group(g, carry):
        base = g * group
        hots, his = [], []
        for j in range(group):
            local = cell_ref[pl.ds(base + j, 1), :] - first
            low_row = jnp.broadcast_to((local % LOW).astype(F32), (LOW, lanes)).astype(BF16)
            his.append(local // LOW)
            hots.append(jnp.where(low_row == iota_low, BF16(1), BF16(0)))
        hot = jnp.concatenate(hots, axis=1)
        hot = jnp.concatenate([hot, hot], axis=0)
        picked = jnp.dot(table_ref[...].astype(BF16), hot, preferred_element_type=F32)
        for j in range(group):
            part = slice(j * lanes, (j + 1) * lanes)
            high_row = jnp.broadcast_to(his[j], (16, lanes))
            high_half = jnp.broadcast_to(his[j], (2 * half, lanes)) - second
            looked = jnp.where(high_row == 0, picked[0:16, part], 0.0)
            for h in range(1, high):
                looked = jnp.where(high_row == h, picked[h * 16 : h * 16 + 16, part], looked)
            rest = jnp.zeros((2 * half, lanes), F32)
            for h in range(0, high, 2):
                top = 16 * high + half * h
                rest = jnp.where(high_half == h, picked[top : top + 2 * half, part], rest)
            rest = rest + pltpu.roll(rest, half, 0)
            looked = jnp.concatenate([looked, rest], axis=0)
            decay = jnp.exp(-rate_ref[pl.ds(base + j, 1), :])
            c = flat[pl.ds(base + j, species, stride=blocks), :]
            c = jnp.concatenate([c, c[16:]], axis=0)
            state_ref[base + j] = looked + (c - looked) * decay
        return carry

    lax.fori_loop(0, blocks // group, mix_group, 0)
    state_ref[blocks] = jnp.zeros((rows, lanes), F32)
    length = length_ref[0]

    def section(s, carry):
        ids = [sched_ref[j * length + s] for j in range(slots)]
        held = []
        for c in range(0, slots, chunk):
            x = jnp.concatenate([state_ref[ids[c + j]] for j in range(chunk)], axis=1)
            upper, lower = split_in_two(x)
            k1 = jnp.concatenate([upper, lower, upper[:16]], axis=0).astype(BF16)
            t = jnp.tanh(jnp.dot(rates_ref[...], k1, preferred_element_type=F32))
            held.append((x, jnp.concatenate(split_in_two(t), axis=0).astype(BF16)))
        for c in range(0, slots, chunk):
            x, k2 = held[c // chunk]
            for p in range(0, chunk, 2):
                pair = (ids[c + p], ids[c + p + 1])
                net = jnp.concatenate([net_ref[batch_ref[i]] for i in pair], axis=0)
                f = jnp.dot(net, k2[:, p * lanes : (p + 2) * lanes], preferred_element_type=F32)
                for i in range(2):
                    cols = slice(i * lanes, (i + 1) * lanes)
                    top = 2 * i * rows
                    change = f[top : top + rows, cols] + f[top + rows : top + 2 * rows, cols]
                    state_ref[pair[i]] = x[:, (p + i) * lanes : (p + i + 1) * lanes] + STEP * change
        return carry

    lax.fori_loop(0, length, section, 0)

    def put_out(g, carry):
        for j in range(group):
            out_flat[pl.ds(g * group + j, species, stride=blocks), :] = state_ref[g * group + j, :species, :]
        return carry

    lax.fori_loop(0, blocks // group, put_out, 0)


def react(length, sched, batch, place, own, near, far, comp, rate, cell, rates, net, slots):
    species, blocks, lanes = comp.shape
    rows = round_up(species + 1, 8)
    high = 3 * (own.shape[0] * lanes // (species + 1)) // LOW
    vmem = pl.BlockSpec(memory_space=pltpu.VMEM)
    return pl.pallas_call(
        functools.partial(react_kernel, group=min(16, blocks), slots=slots, chunk=8),
        out_shape=jax.ShapeDtypeStruct(comp.shape, F32),
        grid_spec=pltpu.PrefetchScalarGridSpec(
            num_scalar_prefetch=4,
            grid=(),
            in_specs=[vmem] * 8,
            out_specs=vmem,
            scratch_shapes=[
                pltpu.VMEM((species * high, 2 * LOW), F32),
                pltpu.VMEM((blocks + 1, rows, lanes), F32),
            ],
        ),
        compiler_params=pltpu.CompilerParams(vmem_limit_bytes=28 << 20),
        cost_estimate=pl.CostEstimate(
            flops=2 * blocks * lanes * high * LOW * 2 * rows, bytes_accessed=8 * comp.size, transcendentals=0
        ),
        name="react",
    )(length, sched, batch, place, own, near, far, comp, rate, cell, rates, net)


def split_two(values):
    upper = lax.reduce_precision(values, 8, 7)
    return upper, lax.reduce_precision(values - upper, 8, 7)


def pack_rates(rates, rows, steps):
    reactions, species = rates.shape
    spare = 2 * species - rows
    upper, lower = split_two(jnp.pad(rates, ((0, steps - reactions), (0, 0))))
    zeros = jnp.zeros((steps, rows - species), F32)
    return jnp.concatenate([upper, lower[:, spare:], upper, zeros, lower[:, :spare]], axis=1).astype(BF16)


def pack_net(inverse, stoichiometry, rows, steps):
    species = inverse.shape[1]
    reactions = stoichiometry.shape[1]
    inverse = jnp.concatenate([inverse, inverse[:, 2 * species - rows :]], axis=1)
    stoichiometry = jnp.pad(stoichiometry, ((0, 0), (0, steps - reactions)))
    net = jnp.einsum("qij,jr->qir", inverse, stoichiometry, precision=lax.Precision.HIGHEST)
    upper, lower = split_two(net)
    return jnp.concatenate(
        [jnp.concatenate([upper, upper], axis=2), jnp.concatenate([lower, jnp.zeros_like(lower)], axis=2)],
        axis=1,
    ).astype(BF16)


def section_schedule(counts, slots):
    blocks = counts.shape[0]
    ids = jnp.arange(blocks, dtype=jnp.int32)
    ends = jnp.sum(jnp.where(ids[None, :] <= ids[:, None], counts[None, :], 0), axis=1)
    total = jnp.sum(counts)
    length = jnp.maximum(jnp.max(counts), (total + slots - 1) // slots)
    places = jnp.arange(round_up(SMAX * blocks + slots, 128), dtype=jnp.int32)
    sched = jnp.sum((ends[:, None] <= places[None, :]).astype(jnp.int32), axis=0)
    return length.reshape(1).astype(jnp.int32), sched


def flat_inverses(inverses, lanes):
    count = inverses.shape[0]
    size = inverses.shape[1] * inverses.shape[2]
    flat = jnp.pad(inverses.reshape(count, size), ((0, 0), (0, round_up(size, lanes) - size)))
    return flat.reshape(-1, lanes)


def from_partner(values, turn, bits):
    slabs, columns = lax.axis_size("gx"), lax.axis_size("yz")
    pairs = []
    for slab in range(slabs):
        bit = bits[(turn - slab % 2) % len(bits)]
        pairs += [(slab * columns + c, slab * columns + (c ^ bit)) for c in range(columns)]
    return lax.ppermute(values, ("gx", "yz"), pairs)


def swap_pairs(near, far):
    count = lax.axis_size("gx")
    first = [(i, i ^ 1) for i in range(count) if i ^ 1 < count]
    second = [(i, i - 1 if i % 2 == 0 else i + 1) for i in range(count)]
    second = [(i, j) for i, j in second if 0 <= j < count]
    return lax.ppermute(near, "gx", first), lax.ppermute(far, "gx", second)


def local(
    composition, particle_mass, mixing_rate, cell_index, section_counts, block_shuffle,
    batch_inverse, rate_exponents, stoichiometry,
):
    blocks, species, lanes = composition.shape
    reactions = rate_exponents.shape[0]
    slabs, columns = lax.axis_size("gx"), lax.axis_size("yz")
    devices = slabs * columns
    slab_cells = CELL_DEV * columns
    rows = round_up(species + 1, 8)
    steps = round_up(reactions, 8)
    slab, column = lax.axis_index("gx"), lax.axis_index("yz")
    odd = slab % 2
    place = jnp.stack([(slab - 1) * slab_cells, 1 - odd, odd]).astype(jnp.int32)

    inverses = [batch_inverse]
    for distance in range(1, slabs):
        inverses.append(lax.ppermute(batch_inverse, "gx", [(i, i ^ distance) for i in range(slabs)]))
    bits = [1 << k for k in range((columns - 1).bit_length())]
    comp = jnp.transpose(composition, (1, 0, 2))
    held = [pltpu.with_memory_space_constraint(v, pltpu.HBM) for v in (comp, particle_mass, cell_index)]
    sides = moments(place, *held, slab_cells, rows, (0, 2))
    near, far = sides[0], sides[1]
    got_near, got_far = swap_pairs(near, far)
    inverses = flat_inverses(jnp.concatenate(inverses, axis=0), lanes)
    own = moments(place, *held, slab_cells, rows, (1,))[0] + got_near + got_far
    sums = own.shape[0]
    for turn in range(len(bits)):
        got = from_partner(jnp.concatenate([own, inverses], axis=0), turn, bits)
        own = own + got[:sums]
        inverses = jnp.concatenate([inverses, got[sums:]], axis=0)
    near, far = swap_pairs(own, own)

    block_ids = jnp.arange(blocks, dtype=jnp.int32)
    slots = min(32, blocks)
    length, sched = section_schedule(section_counts, slots)
    slot = jnp.sum(
        jnp.where(block_shuffle[0][:, None] == block_ids[None, :], block_ids[:, None], 0), axis=0
    )
    batch = (slot // (blocks // devices)) ^ (slab * columns + column)
    turned = batch % columns
    turned = jnp.where(odd == 1, (2 * turned + turned // bits[-1]) % columns, turned)
    batch = turned * slabs + batch // columns
    batch = jnp.pad(batch, (0, 128))
    size = species * species
    matrices = inverses.reshape(devices, -1)[:, :size].reshape(devices, species, species)
    rates = pack_rates(rate_exponents, rows, steps)
    net = pack_net(matrices, stoichiometry, rows, steps)
    out = react(
        length, sched, batch, place, own, near, far, comp, mixing_rate, cell_index, rates, net, slots
    )
    return jnp.transpose(out, (1, 0, 2))


def solution(mesh):
    both = ("gx", "yz")
    in_specs = (
        P(both, None, None),
        P(both, None),
        P(both, None),
        P(both, None),
        P(both),
        P(both, None),
        P(both, None, None),
        P(),
        P(),
    )
    return jax.shard_map(
        local, mesh=mesh, in_specs=in_specs, out_specs=P(both, None, None), check_vma=False
    )
```

```python
import functools

import jax
import jax.numpy as jnp
from jax import lax
from jax.experimental import pallas as pl
from jax.experimental.pallas import tpu as pltpu
from jax.sharding import PartitionSpec as P


STEP = 0.25
CELL_DEV = 128
SMAX = 6
LOW = 256
BF16 = jnp.bfloat16
F32 = jnp.float32


def round_up(value, multiple):
    return -(-value // multiple) * multiple


def split_in_two(values):
    upper = values.astype(BF16).astype(F32)
    return upper, values - upper


def moments_kernel(place_ref, comp_ref, mass_ref, cell_ref, out_ref, acc_ref, *, high, rows):
    step = pl.program_id(0)
    species, step_blocks, lanes = comp_ref.shape
    flat = comp_ref.reshape(species * step_blocks, lanes)

    @pl.when(step == 0)
    def _():
        acc_ref[...] = jnp.zeros_like(acc_ref)

    iota_low = lax.broadcasted_iota(jnp.int32, (LOW, lanes), 0).astype(F32).astype(BF16)
    local = cell_ref[...] - place_ref[0]
    hi = (local // LOW).astype(F32)
    lo = (local % LOW).astype(F32)
    zeros = jnp.zeros((rows - species - 1, lanes), F32)
    tables, spreads = [], []
    for b in range(step_blocks):
        m = mass_ref[b : b + 1, :]
        w = flat[pl.ds(b, species, stride=step_blocks), :] * m
        v = jnp.concatenate([w, m, zeros], axis=0)
        upper = v.astype(BF16).astype(F32)
        pieces = jnp.concatenate([upper, v - upper], axis=0).astype(BF16)
        low_row = jnp.broadcast_to(lo[b : b + 1, :], (LOW, lanes)).astype(BF16)
        tables.append(jnp.where(low_row == iota_low, BF16(1), BF16(0)))
        high_row = jnp.broadcast_to(hi[b : b + 1, :], (2 * rows, lanes)).astype(BF16)
        spreads.append(
            jnp.concatenate(
                [jnp.where(high_row == BF16(h), pieces, BF16(0)) for h in range(high)], axis=0
            )
        )
    table = jnp.concatenate(tables, axis=1)
    spread = jnp.concatenate(spreads, axis=1)
    acc_ref[...] += lax.dot_general(
        spread, table, (((1,), (1,)), ((), ())), preferred_element_type=F32
    )

    @pl.when(step == pl.num_programs(0) - 1)
    def _():
        per = high // 3
        width = per * LOW // lanes
        kept = species + 1
        out_flat = out_ref.reshape(3 * kept * width, lanes)
        for h in range(high):
            top = h * 2 * rows
            slab = h // per
            slot = 0 if slab == 1 else place_ref[1 + slab // 2]
            for c in range(LOW // lanes):
                cols = slice(c * lanes, (c + 1) * lanes)
                total = acc_ref[top : top + rows, cols] + acc_ref[top + rows : top + 2 * rows, cols]
                start = slot * kept * width + (h % per) * (LOW // lanes) + c
                out_flat[pl.ds(start, kept, stride=width), :] = total[:kept]


def moments(place, comp, mass, cell, slab_cells, rows):
    species, blocks, lanes = comp.shape
    high = 3 * slab_cells // LOW
    step_blocks = min(64, blocks)
    sums = (species + 1) * slab_cells // lanes
    return pl.pallas_call(
        functools.partial(moments_kernel, high=high, rows=rows),
        out_shape=jax.ShapeDtypeStruct((3, sums, lanes), F32),
        grid_spec=pltpu.PrefetchScalarGridSpec(
            num_scalar_prefetch=1,
            grid=(blocks // step_blocks,),
            in_specs=[
                pl.BlockSpec((species, step_blocks, lanes), lambda s, p: (0, s, 0)),
                pl.BlockSpec((step_blocks, lanes), lambda s, p: (s, 0)),
                pl.BlockSpec((step_blocks, lanes), lambda s, p: (s, 0)),
            ],
            out_specs=pl.BlockSpec((3, sums, lanes), lambda s, p: (0, 0, 0)),
            scratch_shapes=[pltpu.VMEM((2 * rows * high, LOW), F32)],
        ),
        compiler_params=pltpu.CompilerParams(vmem_limit_bytes=48 << 20),
        cost_estimate=pl.CostEstimate(
            flops=2 * blocks * lanes * high * LOW * 2 * rows, bytes_accessed=4 * comp.size, transcendentals=0
        ),
        name="moments",
    )(place, comp, mass, cell)


def react_kernel(
    length_ref, sched_ref, batch_ref, place_ref,
    own_ref, near_ref, far_ref, comp_ref, rate_ref, cell_ref, rates_ref, net_ref,
    out_ref, table_ref, state_ref, *, group, slots, chunk,
):
    species, blocks, lanes = comp_ref.shape
    width = own_ref.shape[0] // (species + 1)
    rows = state_ref.shape[1]
    flat = comp_ref.reshape(species * blocks, lanes)
    out_flat = out_ref.reshape(species * blocks, lanes)
    parts = LOW // lanes
    per = width // parts
    high = 3 * per
    first = place_ref[0]
    left_near = place_ref[1] == 1
    half = rows - species

    for h in range(high):
        slab = h // per

        def cells(ref):
            start = (h % per) * parts
            return jnp.concatenate(
                [ref[pl.ds(start + c, species + 1, stride=width), :] for c in range(parts)], axis=1
            )

        if slab == 1:
            t = cells(own_ref)
        elif slab == 0:
            t = jnp.where(left_near, cells(near_ref), cells(far_ref))
        else:
            t = jnp.where(left_near, cells(far_ref), cells(near_ref))
        m = t[species : species + 1, :]
        mean = jnp.where(m > 0, t[:species] / m, 0.0)
        for side, piece in enumerate(split_in_two(mean)):
            top = side * species * high
            table_ref[top + h * 16 : top + h * 16 + 16] = piece[:16]
            rest_top = top + 16 * high + half * h
            table_ref[rest_top : rest_top + half] = piece[16:]

    iota_low = lax.broadcasted_iota(jnp.int32, (LOW, lanes), 0).astype(F32).astype(BF16)

    second = lax.broadcasted_iota(jnp.int32, (2 * half, lanes), 0) // half

    def mix_group(g, carry):
        base = g * group
        hots, his = [], []
        for j in range(group):
            local = cell_ref[pl.ds(base + j, 1), :] - first
            low_row = jnp.broadcast_to((local % LOW).astype(F32), (LOW, lanes)).astype(BF16)
            his.append(local // LOW)
            hots.append(jnp.where(low_row == iota_low, BF16(1), BF16(0)))
        hot = jnp.concatenate(hots, axis=1)
        picked = jnp.dot(table_ref[...].astype(BF16), hot, preferred_element_type=F32)
        picked = picked[: species * high] + picked[species * high :]
        for j in range(group):
            part = slice(j * lanes, (j + 1) * lanes)
            high_row = jnp.broadcast_to(his[j], (16, lanes))
            high_half = jnp.broadcast_to(his[j], (2 * half, lanes)) - second
            looked = jnp.where(high_row == 0, picked[0:16, part], 0.0)
            for h in range(1, high):
                looked = jnp.where(high_row == h, picked[h * 16 : h * 16 + 16, part], looked)
            rest = jnp.zeros((2 * half, lanes), F32)
            for h in range(0, high, 2):
                top = 16 * high + half * h
                rest = jnp.where(high_half == h, picked[top : top + 2 * half, part], rest)
            rest = rest + pltpu.roll(rest, half, 0)
            looked = jnp.concatenate([looked, rest], axis=0)
            decay = jnp.exp(-rate_ref[pl.ds(base + j, 1), :])
            c = flat[pl.ds(base + j, species, stride=blocks), :]
            c = jnp.concatenate([c, c[16:]], axis=0)
            state_ref[base + j] = looked + (c - looked) * decay
        return carry

    lax.fori_loop(0, blocks // group, mix_group, 0)
    state_ref[blocks] = jnp.zeros((rows, lanes), F32)
    length = length_ref[0]

    def section(s, carry):
        ids = [sched_ref[j * length + s] for j in range(slots)]
        held = []
        for c in range(0, slots, chunk):
            x = jnp.concatenate([state_ref[ids[c + j]] for j in range(chunk)], axis=1)
            upper, lower = split_in_two(x)
            k1 = jnp.concatenate([upper, lower, upper[:16]], axis=0).astype(BF16)
            t = jnp.tanh(jnp.dot(rates_ref[...], k1, preferred_element_type=F32))
            held.append((x, jnp.concatenate(split_in_two(t), axis=0).astype(BF16)))
        for c in range(0, slots, chunk):
            x, k2 = held[c // chunk]
            for p in range(0, chunk, 2):
                pair = (ids[c + p], ids[c + p + 1])
                net = jnp.concatenate([net_ref[batch_ref[i]] for i in pair], axis=0)
                f = jnp.dot(net, k2[:, p * lanes : (p + 2) * lanes], preferred_element_type=F32)
                for i in range(2):
                    cols = slice(i * lanes, (i + 1) * lanes)
                    top = 2 * i * rows
                    change = f[top : top + rows, cols] + f[top + rows : top + 2 * rows, cols]
                    state_ref[pair[i]] = x[:, (p + i) * lanes : (p + i + 1) * lanes] + STEP * change
        return carry

    lax.fori_loop(0, length, section, 0)

    def put_out(g, carry):
        for j in range(group):
            out_flat[pl.ds(g * group + j, species, stride=blocks), :] = state_ref[g * group + j, :species, :]
        return carry

    lax.fori_loop(0, blocks // group, put_out, 0)


def react(length, sched, batch, place, own, near, far, comp, rate, cell, rates, net, slots):
    species, blocks, lanes = comp.shape
    rows = round_up(species + 1, 8)
    high = 3 * (own.shape[0] * lanes // (species + 1)) // LOW
    vmem = pl.BlockSpec(memory_space=pltpu.VMEM)
    return pl.pallas_call(
        functools.partial(react_kernel, group=min(128, blocks), slots=slots, chunk=8),
        out_shape=jax.ShapeDtypeStruct(comp.shape, F32),
        grid_spec=pltpu.PrefetchScalarGridSpec(
            num_scalar_prefetch=4,
            grid=(),
            in_specs=[vmem] * 8,
            out_specs=vmem,
            scratch_shapes=[
                pltpu.VMEM((2 * species * high, LOW), F32),
                pltpu.VMEM((blocks + 1, rows, lanes), F32),
            ],
        ),
        compiler_params=pltpu.CompilerParams(vmem_limit_bytes=28 << 20),
        cost_estimate=pl.CostEstimate(
            flops=2 * blocks * lanes * high * LOW * 2 * rows, bytes_accessed=8 * comp.size, transcendentals=0
        ),
        name="react",
    )(length, sched, batch, place, own, near, far, comp, rate, cell, rates, net)


def split_two(values):
    upper = lax.reduce_precision(values, 8, 7)
    return upper, lax.reduce_precision(values - upper, 8, 7)


def pack_rates(rates, rows, steps):
    reactions, species = rates.shape
    spare = 2 * species - rows
    upper, lower = split_two(jnp.pad(rates, ((0, steps - reactions), (0, 0))))
    zeros = jnp.zeros((steps, rows - species), F32)
    return jnp.concatenate([upper, lower[:, spare:], upper, zeros, lower[:, :spare]], axis=1).astype(BF16)


def pack_net(inverse, stoichiometry, rows, steps):
    species = inverse.shape[1]
    reactions = stoichiometry.shape[1]
    inverse = jnp.concatenate([inverse, inverse[:, 2 * species - rows :]], axis=1)
    stoichiometry = jnp.pad(stoichiometry, ((0, 0), (0, steps - reactions)))
    net = jnp.einsum("qij,jr->qir", inverse, stoichiometry, precision=lax.Precision.HIGHEST)
    upper, lower = split_two(net)
    return jnp.concatenate(
        [jnp.concatenate([upper, upper], axis=2), jnp.concatenate([lower, jnp.zeros_like(lower)], axis=2)],
        axis=1,
    ).astype(BF16)


def section_schedule(counts, slots):
    blocks = counts.shape[0]
    ids = jnp.arange(blocks, dtype=jnp.int32)
    ends = jnp.sum(jnp.where(ids[None, :] <= ids[:, None], counts[None, :], 0), axis=1)
    total = jnp.sum(counts)
    length = jnp.maximum(jnp.max(counts), (total + slots - 1) // slots)
    places = jnp.arange(round_up(SMAX * blocks + slots, 128), dtype=jnp.int32)
    sched = jnp.sum((ends[:, None] <= places[None, :]).astype(jnp.int32), axis=0)
    return length.reshape(1).astype(jnp.int32), sched


def flat_inverses(inverses, lanes):
    count = inverses.shape[0]
    size = inverses.shape[1] * inverses.shape[2]
    flat = jnp.pad(inverses.reshape(count, size), ((0, 0), (0, round_up(size, lanes) - size)))
    return flat.reshape(-1, lanes)


def from_partner(values, mask):
    count = lax.axis_size("yz")
    return lax.ppermute(values, "yz", [(i, i ^ mask) for i in range(count)])


def swap_pairs(near, far):
    count = lax.axis_size("gx")
    first = [(i, i ^ 1) for i in range(count) if i ^ 1 < count]
    second = [(i, i - 1 if i % 2 == 0 else i + 1) for i in range(count)]
    second = [(i, j) for i, j in second if 0 <= j < count]
    near = lax.ppermute(near, "gx", first)
    far = lax.ppermute(far, "gx", second)
    return near, far


def local(
    composition, particle_mass, mixing_rate, cell_index, section_counts, block_shuffle,
    batch_inverse, rate_exponents, stoichiometry,
):
    blocks, species, lanes = composition.shape
    reactions = rate_exponents.shape[0]
    slabs, columns = lax.axis_size("gx"), lax.axis_size("yz")
    devices = slabs * columns
    slab_cells = CELL_DEV * columns
    rows = round_up(species + 1, 8)
    steps = round_up(reactions, 8)
    slab, column = lax.axis_index("gx"), lax.axis_index("yz")
    odd = slab % 2
    place = jnp.stack([(slab - 1) * slab_cells, 2 - odd, 1 + odd]).astype(jnp.int32)

    inverses = [batch_inverse]
    for distance in range(1, slabs):
        inverses.append(lax.ppermute(batch_inverse, "gx", [(i, i ^ distance) for i in range(slabs)]))
    bits = [1 << k for k in range((columns - 1).bit_length())]
    comp = jnp.transpose(composition, (1, 0, 2))
    held = [pltpu.with_memory_space_constraint(v, pltpu.HBM) for v in (comp, particle_mass, cell_index)]
    partial = moments(place, *held, slab_cells, rows)
    near, far = partial[1], partial[2]
    got_near, got_far = swap_pairs(near, far)
    inverses = flat_inverses(jnp.concatenate(inverses, axis=0), lanes)
    own = partial[0] + got_near + got_far
    sums = own.shape[0]
    for at in range(0, len(bits), 2):
        message = jnp.concatenate([own, inverses], axis=0)
        masks = [sum(m) for m in ([bits[at]], bits[at + 1 : at + 2], bits[at : at + 2])]
        got = [from_partner(message, m) for m in (masks if at + 1 < len(bits) else masks[:1])]
        own = sum((g[:sums] for g in got), own)
        inverses = jnp.concatenate([inverses] + [g[sums:] for g in got], axis=0)
    near, far = swap_pairs(own, own)

    block_ids = jnp.arange(blocks, dtype=jnp.int32)
    slots = min(32, blocks)
    length, sched = section_schedule(section_counts, slots)
    slot = jnp.sum(
        jnp.where(block_shuffle[0][:, None] == block_ids[None, :], block_ids[:, None], 0), axis=0
    )
    batch = (slot // (blocks // devices)) ^ (slab * columns + column)
    batch = batch % columns * slabs + batch // columns
    batch = jnp.pad(batch, (0, 128))
    size = species * species
    matrices = inverses.reshape(devices, -1)[:, :size].reshape(devices, species, species)
    rates = pack_rates(rate_exponents, rows, steps)
    net = pack_net(matrices, stoichiometry, rows, steps)
    out = react(
        length, sched, batch, place, own, near, far, comp, mixing_rate, cell_index, rates, net, slots
    )
    return jnp.transpose(out, (1, 0, 2))


def solution(mesh):
    both = ("gx", "yz")
    in_specs = (
        P(both, None, None),
        P(both, None),
        P(both, None),
        P(both, None),
        P(both),
        P(both, None),
        P(both, None, None),
        P(),
        P(),
    )
    return jax.shard_map(local, mesh=mesh, in_specs=in_specs, out_specs=P(both, None, None), check_vma=False)
```

```python
import functools

import jax
import jax.numpy as jnp
from jax import lax
from jax.experimental import pallas as pl
from jax.experimental.pallas import tpu as pltpu
from jax.sharding import PartitionSpec as P


STEP = 0.25
CELL_DEV = 128
SMAX = 6
LOW = 256
BF16 = jnp.bfloat16
F32 = jnp.float32


def round_up(value, multiple):
    return -(-value // multiple) * multiple


def split_in_two(values):
    upper = values.astype(BF16).astype(F32)
    return upper, values - upper


def moments_kernel(place_ref, comp_ref, mass_ref, cell_ref, out_ref, acc_ref, *, high, rows):
    step = pl.program_id(0)
    species, step_blocks, lanes = comp_ref.shape
    flat = comp_ref.reshape(species * step_blocks, lanes)

    @pl.when(step == 0)
    def _():
        acc_ref[...] = jnp.zeros_like(acc_ref)

    iota_low = lax.broadcasted_iota(jnp.int32, (LOW, lanes), 0).astype(F32).astype(BF16)
    local = cell_ref[...] - place_ref[0]
    hi = (local // LOW).astype(F32)
    lo = (local % LOW).astype(F32)
    zeros = jnp.zeros((rows - species - 1, lanes), F32)
    tables, spreads = [], []
    for b in range(step_blocks):
        m = mass_ref[b : b + 1, :]
        w = flat[pl.ds(b, species, stride=step_blocks), :] * m
        v = jnp.concatenate([w, m, zeros], axis=0)
        upper = v.astype(BF16).astype(F32)
        pieces = jnp.concatenate([upper, v - upper], axis=0).astype(BF16)
        low_row = jnp.broadcast_to(lo[b : b + 1, :], (LOW, lanes)).astype(BF16)
        tables.append(jnp.where(low_row == iota_low, BF16(1), BF16(0)))
        high_row = jnp.broadcast_to(hi[b : b + 1, :], (2 * rows, lanes)).astype(BF16)
        spreads.append(
            jnp.concatenate(
                [jnp.where(high_row == BF16(h), pieces, BF16(0)) for h in range(high)], axis=0
            )
        )
    table = jnp.concatenate(tables, axis=1)
    spread = jnp.concatenate(spreads, axis=1)
    acc_ref[...] += lax.dot_general(
        spread, table, (((1,), (1,)), ((), ())), preferred_element_type=F32
    )

    @pl.when(step == pl.num_programs(0) - 1)
    def _():
        per = high // 3
        width = per * LOW // lanes
        kept = species + 1
        out_flat = out_ref.reshape(3 * kept * width, lanes)
        for h in range(high):
            top = h * 2 * rows
            slab = h // per
            slot = 0 if slab == 1 else place_ref[1 + slab // 2]
            for c in range(LOW // lanes):
                cols = slice(c * lanes, (c + 1) * lanes)
                total = acc_ref[top : top + rows, cols] + acc_ref[top + rows : top + 2 * rows, cols]
                start = slot * kept * width + (h % per) * (LOW // lanes) + c
                out_flat[pl.ds(start, kept, stride=width), :] = total[:kept]


def moments(place, comp, mass, cell, slab_cells, rows):
    species, blocks, lanes = comp.shape
    high = 3 * slab_cells // LOW
    step_blocks = min(64, blocks)
    sums = (species + 1) * slab_cells // lanes
    return pl.pallas_call(
        functools.partial(moments_kernel, high=high, rows=rows),
        out_shape=jax.ShapeDtypeStruct((3, sums, lanes), F32),
        grid_spec=pltpu.PrefetchScalarGridSpec(
            num_scalar_prefetch=1,
            grid=(blocks // step_blocks,),
            in_specs=[
                pl.BlockSpec((species, step_blocks, lanes), lambda s, p: (0, s, 0)),
                pl.BlockSpec((step_blocks, lanes), lambda s, p: (s, 0)),
                pl.BlockSpec((step_blocks, lanes), lambda s, p: (s, 0)),
            ],
            out_specs=pl.BlockSpec((3, sums, lanes), lambda s, p: (0, 0, 0)),
            scratch_shapes=[pltpu.VMEM((2 * rows * high, LOW), F32)],
        ),
        compiler_params=pltpu.CompilerParams(vmem_limit_bytes=48 << 20),
        cost_estimate=pl.CostEstimate(
            flops=2 * blocks * lanes * high * LOW * 2 * rows, bytes_accessed=4 * comp.size, transcendentals=0
        ),
        name="moments",
    )(place, comp, mass, cell)


def react_kernel(
    length_ref, sched_ref, batch_ref, place_ref,
    own_ref, near_ref, far_ref, comp_ref, rate_ref, cell_ref, rates_ref, net_ref,
    out_ref, table_ref, state_ref, sem_ref, *, group, slots, chunk,
):
    species, blocks, lanes = comp_ref.shape
    width = own_ref.shape[0] // (species + 1)
    rows = state_ref.shape[1]
    flat = comp_ref.reshape(species * blocks, lanes)
    parts = LOW // lanes
    per = width // parts
    high = 3 * per
    first = place_ref[0]
    left_near = place_ref[1] == 1
    half = rows - species

    for h in range(high):
        slab = h // per

        def cells(ref):
            start = (h % per) * parts
            return jnp.concatenate(
                [ref[pl.ds(start + c, species + 1, stride=width), :] for c in range(parts)], axis=1
            )

        if slab == 1:
            t = cells(own_ref)
        elif slab == 0:
            t = jnp.where(left_near, cells(near_ref), cells(far_ref))
        else:
            t = jnp.where(left_near, cells(far_ref), cells(near_ref))
        m = t[species : species + 1, :]
        mean = jnp.where(m > 0, t[:species] / m, 0.0)
        for side, piece in enumerate(split_in_two(mean)):
            top = side * species * high
            table_ref[top + h * 16 : top + h * 16 + 16] = piece[:16]
            rest_top = top + 16 * high + half * h
            table_ref[rest_top : rest_top + half] = piece[16:]

    iota_low = lax.broadcasted_iota(jnp.int32, (LOW, lanes), 0).astype(F32).astype(BF16)

    second = lax.broadcasted_iota(jnp.int32, (2 * half, lanes), 0) // half

    def mix_group(g, carry):
        base = g * group
        hots, his = [], []
        for j in range(group):
            local = cell_ref[pl.ds(base + j, 1), :] - first
            low_row = jnp.broadcast_to((local % LOW).astype(F32), (LOW, lanes)).astype(BF16)
            his.append(local // LOW)
            hots.append(jnp.where(low_row == iota_low, BF16(1), BF16(0)))
        hot = jnp.concatenate(hots, axis=1)
        picked = jnp.dot(table_ref[...].astype(BF16), hot, preferred_element_type=F32)
        picked = picked[: species * high] + picked[species * high :]
        for j in range(group):
            part = slice(j * lanes, (j + 1) * lanes)
            high_row = jnp.broadcast_to(his[j], (16, lanes))
            high_half = jnp.broadcast_to(his[j], (2 * half, lanes)) - second
            looked = jnp.where(high_row == 0, picked[0:16, part], 0.0)
            for h in range(1, high):
                looked = jnp.where(high_row == h, picked[h * 16 : h * 16 + 16, part], looked)
            rest = jnp.zeros((2 * half, lanes), F32)
            for h in range(0, high, 2):
                top = 16 * high + half * h
                rest = jnp.where(high_half == h, picked[top : top + 2 * half, part], rest)
            rest = rest + pltpu.roll(rest, half, 0)
            looked = jnp.concatenate([looked, rest], axis=0)
            decay = jnp.exp(-rate_ref[pl.ds(base + j, 1), :])
            c = flat[pl.ds(base + j, species, stride=blocks), :]
            c = jnp.concatenate([c, c[16:]], axis=0)
            state_ref[base + j] = looked + (c - looked) * decay
        return carry

    lax.fori_loop(0, blocks // group, mix_group, 0)
    state_ref[blocks] = jnp.zeros((rows, lanes), F32)
    length = length_ref[0]

    def section(s, carry):
        ids = [sched_ref[j * length + s] for j in range(slots)]
        held = []
        for c in range(0, slots, chunk):
            x = jnp.concatenate([state_ref[ids[c + j]] for j in range(chunk)], axis=1)
            upper, lower = split_in_two(x)
            k1 = jnp.concatenate([upper, lower, upper[:16]], axis=0).astype(BF16)
            t = jnp.tanh(jnp.dot(rates_ref[...], k1, preferred_element_type=F32))
            held.append((x, jnp.concatenate(split_in_two(t), axis=0).astype(BF16)))
        for c in range(0, slots, chunk):
            x, k2 = held[c // chunk]
            for p in range(0, chunk, 2):
                pair = (ids[c + p], ids[c + p + 1])
                net = jnp.concatenate([net_ref[batch_ref[i]] for i in pair], axis=0)
                f = jnp.dot(net, k2[:, p * lanes : (p + 2) * lanes], preferred_element_type=F32)
                for i in range(2):
                    cols = slice(i * lanes, (i + 1) * lanes)
                    top = 2 * i * rows
                    change = f[top : top + rows, cols] + f[top + rows : top + 2 * rows, cols]
                    state_ref[pair[i]] = x[:, (p + i) * lanes : (p + i + 1) * lanes] + STEP * change
        return carry

    lax.fori_loop(0, length, section, 0)

    copies = [
        pltpu.make_async_copy(state_ref.at[pl.ds(0, blocks), n, :], out_ref.at[n], sem_ref.at[n])
        for n in range(species)
    ]
    for copy in copies:
        copy.start()
    for copy in copies:
        copy.wait()


def react(length, sched, batch, place, own, near, far, comp, rate, cell, rates, net, slots):
    species, blocks, lanes = comp.shape
    rows = round_up(species + 1, 8)
    high = 3 * (own.shape[0] * lanes // (species + 1)) // LOW
    vmem = pl.BlockSpec(memory_space=pltpu.VMEM)
    return pl.pallas_call(
        functools.partial(react_kernel, group=min(128, blocks), slots=slots, chunk=8),
        out_shape=jax.ShapeDtypeStruct(comp.shape, F32),
        grid_spec=pltpu.PrefetchScalarGridSpec(
            num_scalar_prefetch=4,
            grid=(),
            in_specs=[vmem] * 8,
            out_specs=pl.BlockSpec(memory_space=pltpu.HBM),
            scratch_shapes=[
                pltpu.VMEM((2 * species * high, LOW), F32),
                pltpu.VMEM((blocks + 1, rows, lanes), F32),
                pltpu.SemaphoreType.DMA((species,)),
            ],
        ),
        compiler_params=pltpu.CompilerParams(vmem_limit_bytes=28 << 20),
        cost_estimate=pl.CostEstimate(
            flops=2 * blocks * lanes * high * LOW * 2 * rows, bytes_accessed=8 * comp.size, transcendentals=0
        ),
        name="react",
    )(length, sched, batch, place, own, near, far, comp, rate, cell, rates, net)


def split_two(values):
    upper = lax.reduce_precision(values, 8, 7)
    return upper, lax.reduce_precision(values - upper, 8, 7)


def pack_rates(rates, rows, steps):
    reactions, species = rates.shape
    spare = 2 * species - rows
    upper, lower = split_two(jnp.pad(rates, ((0, steps - reactions), (0, 0))))
    zeros = jnp.zeros((steps, rows - species), F32)
    return jnp.concatenate([upper, lower[:, spare:], upper, zeros, lower[:, :spare]], axis=1).astype(BF16)


def pack_net(inverse, stoichiometry, rows, steps):
    species = inverse.shape[1]
    reactions = stoichiometry.shape[1]
    inverse = jnp.concatenate([inverse, inverse[:, 2 * species - rows :]], axis=1)
    stoichiometry = jnp.pad(stoichiometry, ((0, 0), (0, steps - reactions)))
    net = jnp.einsum("qij,jr->qir", inverse, stoichiometry, precision=lax.Precision.HIGHEST)
    upper, lower = split_two(net)
    return jnp.concatenate(
        [jnp.concatenate([upper, upper], axis=2), jnp.concatenate([lower, jnp.zeros_like(lower)], axis=2)],
        axis=1,
    ).astype(BF16)


def section_schedule(counts, slots):
    blocks = counts.shape[0]
    ids = jnp.arange(blocks, dtype=jnp.int32)
    ends = jnp.sum(jnp.where(ids[None, :] <= ids[:, None], counts[None, :], 0), axis=1)
    total = jnp.sum(counts)
    length = jnp.maximum(jnp.max(counts), (total + slots - 1) // slots)
    places = jnp.arange(round_up(SMAX * blocks + slots, 128), dtype=jnp.int32)
    sched = jnp.sum((ends[:, None] <= places[None, :]).astype(jnp.int32), axis=0)
    return length.reshape(1).astype(jnp.int32), sched


def flat_inverses(inverses, lanes):
    count = inverses.shape[0]
    size = inverses.shape[1] * inverses.shape[2]
    flat = jnp.pad(inverses.reshape(count, size), ((0, 0), (0, round_up(size, lanes) - size)))
    return flat.reshape(-1, lanes)


def from_partner(values, mask):
    count = lax.axis_size("yz")
    return lax.ppermute(values, "yz", [(i, i ^ mask) for i in range(count)])


def swap_pairs(near, far):
    count = lax.axis_size("gx")
    first = [(i, i ^ 1) for i in range(count) if i ^ 1 < count]
    second = [(i, i - 1 if i % 2 == 0 else i + 1) for i in range(count)]
    second = [(i, j) for i, j in second if 0 <= j < count]
    near = lax.ppermute(near, "gx", first)
    far = lax.ppermute(far, "gx", second)
    return near, far


def local(
    composition, particle_mass, mixing_rate, cell_index, section_counts, block_shuffle,
    batch_inverse, rate_exponents, stoichiometry,
):
    blocks, species, lanes = composition.shape
    reactions = rate_exponents.shape[0]
    slabs, columns = lax.axis_size("gx"), lax.axis_size("yz")
    devices = slabs * columns
    slab_cells = CELL_DEV * columns
    rows = round_up(species + 1, 8)
    steps = round_up(reactions, 8)
    slab, column = lax.axis_index("gx"), lax.axis_index("yz")
    odd = slab % 2
    place = jnp.stack([(slab - 1) * slab_cells, 2 - odd, 1 + odd]).astype(jnp.int32)

    inverses = [batch_inverse]
    for distance in range(1, slabs):
        inverses.append(lax.ppermute(batch_inverse, "gx", [(i, i ^ distance) for i in range(slabs)]))
    bits = [1 << k for k in range((columns - 1).bit_length())]
    comp = jnp.transpose(composition, (1, 0, 2))
    held = [pltpu.with_memory_space_constraint(v, pltpu.HBM) for v in (comp, particle_mass, cell_index)]
    partial = moments(place, *held, slab_cells, rows)
    near, far = partial[1], partial[2]
    got_near, got_far = swap_pairs(near, far)
    inverses = flat_inverses(jnp.concatenate(inverses, axis=0), lanes)
    own = partial[0] + got_near + got_far
    sums = own.shape[0]
    for at in range(0, len(bits), 2):
        message = jnp.concatenate([own, inverses], axis=0)
        masks = [sum(m) for m in ([bits[at]], bits[at + 1 : at + 2], bits[at : at + 2])]
        got = [from_partner(message, m) for m in (masks if at + 1 < len(bits) else masks[:1])]
        own = sum((g[:sums] for g in got), own)
        inverses = jnp.concatenate([inverses] + [g[sums:] for g in got], axis=0)
    near, far = swap_pairs(own, own)

    block_ids = jnp.arange(blocks, dtype=jnp.int32)
    slots = min(32, blocks)
    length, sched = section_schedule(section_counts, slots)
    slot = jnp.sum(
        jnp.where(block_shuffle[0][:, None] == block_ids[None, :], block_ids[:, None], 0), axis=0
    )
    batch = (slot // (blocks // devices)) ^ (slab * columns + column)
    batch = batch % columns * slabs + batch // columns
    batch = jnp.pad(batch, (0, 128))
    size = species * species
    matrices = inverses.reshape(devices, -1)[:, :size].reshape(devices, species, species)
    rates = pack_rates(rate_exponents, rows, steps)
    net = pack_net(matrices, stoichiometry, rows, steps)
    out = react(
        length, sched, batch, place, own, near, far, comp, mixing_rate, cell_index, rates, net, slots
    )
    return jnp.transpose(out, (1, 0, 2))


def solution(mesh):
    both = ("gx", "yz")
    in_specs = (
        P(both, None, None),
        P(both, None),
        P(both, None),
        P(both, None),
        P(both),
        P(both, None),
        P(both, None, None),
        P(),
        P(),
    )
    return jax.shard_map(local, mesh=mesh, in_specs=in_specs, out_specs=P(both, None, None), check_vma=False)
```

```python
import functools

import jax
import jax.numpy as jnp
from jax import lax
from jax.experimental import pallas as pl
from jax.experimental.pallas import tpu as pltpu
from jax.sharding import PartitionSpec as P


STEP = 0.25
CELL_DEV = 128
SMAX = 6
LOW = 256
BF16 = jnp.bfloat16
F32 = jnp.float32


def round_up(value, multiple):
    return -(-value // multiple) * multiple


def split_in_two(values):
    upper = values.astype(BF16).astype(F32)
    return upper, values - upper


def moments_kernel(place_ref, comp_ref, mass_ref, cell_ref, out_ref, acc_ref, *, high, rows):
    step = pl.program_id(0)
    species, step_blocks, lanes = comp_ref.shape
    flat = comp_ref.reshape(species * step_blocks, lanes)

    @pl.when(step == 0)
    def _():
        acc_ref[...] = jnp.zeros_like(acc_ref)

    iota_low = lax.broadcasted_iota(jnp.int32, (LOW, lanes), 0).astype(F32).astype(BF16)
    local = cell_ref[...] - place_ref[0]
    hi = (local // LOW).astype(F32)
    lo = (local % LOW).astype(F32)
    zeros = jnp.zeros((rows - species - 1, lanes), F32)
    tables, spreads = [], []
    for b in range(step_blocks):
        m = mass_ref[b : b + 1, :]
        w = flat[pl.ds(b, species, stride=step_blocks), :] * m
        v = jnp.concatenate([w, m, zeros], axis=0)
        upper = v.astype(BF16).astype(F32)
        pieces = jnp.concatenate([upper, v - upper], axis=0).astype(BF16)
        low_row = jnp.broadcast_to(lo[b : b + 1, :], (LOW, lanes)).astype(BF16)
        tables.append(jnp.where(low_row == iota_low, BF16(1), BF16(0)))
        high_row = jnp.broadcast_to(hi[b : b + 1, :], (2 * rows, lanes)).astype(BF16)
        spreads.append(
            jnp.concatenate(
                [jnp.where(high_row == BF16(h), pieces, BF16(0)) for h in range(high)], axis=0
            )
        )
    table = jnp.concatenate(tables, axis=1)
    spread = jnp.concatenate(spreads, axis=1)
    acc_ref[...] += lax.dot_general(
        spread, table, (((1,), (1,)), ((), ())), preferred_element_type=F32
    )

    @pl.when(step == pl.num_programs(0) - 1)
    def _():
        per = high // 3
        width = per * LOW // lanes
        kept = species + 1
        out_flat = out_ref.reshape(3 * kept * width, lanes)
        for h in range(high):
            top = h * 2 * rows
            slab = h // per
            slot = 0 if slab == 1 else place_ref[1 + slab // 2]
            for c in range(LOW // lanes):
                cols = slice(c * lanes, (c + 1) * lanes)
                total = acc_ref[top : top + rows, cols] + acc_ref[top + rows : top + 2 * rows, cols]
                start = slot * kept * width + (h % per) * (LOW // lanes) + c
                out_flat[pl.ds(start, kept, stride=width), :] = total[:kept]


def moments(place, comp, mass, cell, slab_cells, rows):
    species, blocks, lanes = comp.shape
    high = 3 * slab_cells // LOW
    step_blocks = min(64, blocks)
    sums = (species + 1) * slab_cells // lanes
    return pl.pallas_call(
        functools.partial(moments_kernel, high=high, rows=rows),
        out_shape=jax.ShapeDtypeStruct((3, sums, lanes), F32),
        grid_spec=pltpu.PrefetchScalarGridSpec(
            num_scalar_prefetch=1,
            grid=(blocks // step_blocks,),
            in_specs=[
                pl.BlockSpec((species, step_blocks, lanes), lambda s, p: (0, s, 0)),
                pl.BlockSpec((step_blocks, lanes), lambda s, p: (s, 0)),
                pl.BlockSpec((step_blocks, lanes), lambda s, p: (s, 0)),
            ],
            out_specs=pl.BlockSpec((3, sums, lanes), lambda s, p: (0, 0, 0)),
            scratch_shapes=[pltpu.VMEM((2 * rows * high, LOW), F32)],
        ),
        compiler_params=pltpu.CompilerParams(vmem_limit_bytes=48 << 20),
        cost_estimate=pl.CostEstimate(
            flops=2 * blocks * lanes * high * LOW * 2 * rows, bytes_accessed=4 * comp.size, transcendentals=0
        ),
        name="moments",
    )(place, comp, mass, cell)


def react_kernel(
    length_ref, sched_ref, batch_ref, place_ref,
    own_ref, near_ref, far_ref, comp_ref, rate_ref, cell_ref, rates_ref, net_ref,
    out_ref, table_ref, state_ref, sem_ref, *, group, slots, chunk,
):
    species, blocks, lanes = comp_ref.shape
    width = own_ref.shape[0] // (species + 1)
    rows = state_ref.shape[1]
    flat = comp_ref.reshape(species * blocks, lanes)
    parts = LOW // lanes
    per = width // parts
    high = 3 * per
    first = place_ref[0]
    left_near = place_ref[1] == 1
    half = rows - species

    for h in range(high):
        slab = h // per

        def cells(ref):
            start = (h % per) * parts
            return jnp.concatenate(
                [ref[pl.ds(start + c, species + 1, stride=width), :] for c in range(parts)], axis=1
            )

        if slab == 1:
            t = cells(own_ref)
        elif slab == 0:
            t = jnp.where(left_near, cells(near_ref), cells(far_ref))
        else:
            t = jnp.where(left_near, cells(far_ref), cells(near_ref))
        m = t[species : species + 1, :]
        mean = jnp.where(m > 0, t[:species] / m, 0.0)
        for side, piece in enumerate(split_in_two(mean)):
            top = side * species * high
            table_ref[top + h * 16 : top + h * 16 + 16] = piece[:16]
            rest_top = top + 16 * high + half * h
            table_ref[rest_top : rest_top + half] = piece[16:]

    iota_low = lax.broadcasted_iota(jnp.int32, (LOW, lanes), 0).astype(F32).astype(BF16)

    second = lax.broadcasted_iota(jnp.int32, (2 * half, lanes), 0) // half

    def mix_group(g, carry):
        base = g * group
        hots, his = [], []
        for j in range(group):
            local = cell_ref[pl.ds(base + j, 1), :] - first
            low_row = jnp.broadcast_to((local % LOW).astype(F32), (LOW, lanes)).astype(BF16)
            his.append(local // LOW)
            hots.append(jnp.where(low_row == iota_low, BF16(1), BF16(0)))
        hot = jnp.concatenate(hots, axis=1)
        picked = jnp.dot(table_ref[...].astype(BF16), hot, preferred_element_type=F32)
        picked = picked[: species * high] + picked[species * high :]
        for j in range(group):
            part = slice(j * lanes, (j + 1) * lanes)
            high_row = jnp.broadcast_to(his[j], (16, lanes))
            high_half = jnp.broadcast_to(his[j], (2 * half, lanes)) - second
            looked = jnp.where(high_row == 0, picked[0:16, part], 0.0)
            for h in range(1, high):
                looked = jnp.where(high_row == h, picked[h * 16 : h * 16 + 16, part], looked)
            rest = jnp.zeros((2 * half, lanes), F32)
            for h in range(0, high, 2):
                top = 16 * high + half * h
                rest = jnp.where(high_half == h, picked[top : top + 2 * half, part], rest)
            rest = rest + pltpu.roll(rest, half, 0)
            looked = jnp.concatenate([looked, rest], axis=0)
            decay = jnp.exp(-rate_ref[pl.ds(base + j, 1), :])
            c = flat[pl.ds(base + j, species, stride=blocks), :]
            c = jnp.concatenate([c, c[16:]], axis=0)
            state_ref[base + j] = looked + (c - looked) * decay
        return carry

    lax.fori_loop(0, blocks // group, mix_group, 0)
    state_ref[blocks] = jnp.zeros((rows, lanes), F32)
    length = length_ref[0]

    def section(s, carry):
        ids = [sched_ref[j * length + s] for j in range(slots)]
        held = []
        for c in range(0, slots, chunk):
            x = jnp.concatenate([state_ref[ids[c + j]] for j in range(chunk)], axis=1)
            upper, lower = split_in_two(x)
            k1 = jnp.concatenate([upper, lower, upper[:16]], axis=0).astype(BF16)
            t = jnp.tanh(jnp.dot(rates_ref[...], k1, preferred_element_type=F32))
            held.append((x, jnp.concatenate(split_in_two(t), axis=0).astype(BF16)))
        for c in range(0, slots, chunk):
            x, k2 = held[c // chunk]
            for p in range(0, chunk, 2):
                pair = (ids[c + p], ids[c + p + 1])
                net = jnp.concatenate([net_ref[batch_ref[i]] for i in pair], axis=0)
                f = jnp.dot(net, k2[:, p * lanes : (p + 2) * lanes], preferred_element_type=F32)
                for i in range(2):
                    cols = slice(i * lanes, (i + 1) * lanes)
                    top = 2 * i * rows
                    change = f[top : top + rows, cols] + f[top + rows : top + 2 * rows, cols]
                    state_ref[pair[i]] = x[:, (p + i) * lanes : (p + i + 1) * lanes] + STEP * change
        return carry

    lax.fori_loop(0, length, section, 0)

    copies = [
        pltpu.make_async_copy(state_ref.at[pl.ds(0, blocks), n, :], out_ref.at[n], sem_ref.at[n])
        for n in range(species)
    ]
    for copy in copies:
        copy.start()
    for copy in copies:
        copy.wait()


def react(length, sched, batch, place, own, near, far, comp, rate, cell, rates, net, slots):
    species, blocks, lanes = comp.shape
    rows = round_up(species + 1, 8)
    high = 3 * (own.shape[0] * lanes // (species + 1)) // LOW
    vmem = pl.BlockSpec(memory_space=pltpu.VMEM)
    return pl.pallas_call(
        functools.partial(react_kernel, group=min(128, blocks), slots=slots, chunk=4),
        out_shape=jax.ShapeDtypeStruct(comp.shape, F32),
        grid_spec=pltpu.PrefetchScalarGridSpec(
            num_scalar_prefetch=4,
            grid=(),
            in_specs=[vmem] * 8,
            out_specs=pl.BlockSpec(memory_space=pltpu.HBM),
            scratch_shapes=[
                pltpu.VMEM((2 * species * high, LOW), F32),
                pltpu.VMEM((blocks + 1, rows, lanes), F32),
                pltpu.SemaphoreType.DMA((species,)),
            ],
        ),
        compiler_params=pltpu.CompilerParams(vmem_limit_bytes=28 << 20),
        cost_estimate=pl.CostEstimate(
            flops=2 * blocks * lanes * high * LOW * 2 * rows, bytes_accessed=8 * comp.size, transcendentals=0
        ),
        name="react",
    )(length, sched, batch, place, own, near, far, comp, rate, cell, rates, net)


def split_two(values):
    upper = lax.reduce_precision(values, 8, 7)
    return upper, lax.reduce_precision(values - upper, 8, 7)


def pack_rates(rates, rows, steps):
    reactions, species = rates.shape
    spare = 2 * species - rows
    upper, lower = split_two(jnp.pad(rates, ((0, steps - reactions), (0, 0))))
    zeros = jnp.zeros((steps, rows - species), F32)
    return jnp.concatenate([upper, lower[:, spare:], upper, zeros, lower[:, :spare]], axis=1).astype(BF16)


def pack_net(inverse, stoichiometry, rows, steps):
    species = inverse.shape[1]
    reactions = stoichiometry.shape[1]
    inverse = jnp.concatenate([inverse, inverse[:, 2 * species - rows :]], axis=1)
    stoichiometry = jnp.pad(stoichiometry, ((0, 0), (0, steps - reactions)))
    net = jnp.einsum("qij,jr->qir", inverse, stoichiometry, precision=lax.Precision.HIGHEST)
    upper, lower = split_two(net)
    return jnp.concatenate(
        [jnp.concatenate([upper, upper], axis=2), jnp.concatenate([lower, jnp.zeros_like(lower)], axis=2)],
        axis=1,
    ).astype(BF16)


def section_schedule(counts, slots):
    blocks = counts.shape[0]
    ids = jnp.arange(blocks, dtype=jnp.int32)
    ends = jnp.sum(jnp.where(ids[None, :] <= ids[:, None], counts[None, :], 0), axis=1)
    total = jnp.sum(counts)
    length = jnp.maximum(jnp.max(counts), (total + slots - 1) // slots)
    places = jnp.arange(round_up(SMAX * blocks + slots, 128), dtype=jnp.int32)
    sched = jnp.sum((ends[:, None] <= places[None, :]).astype(jnp.int32), axis=0)
    return length.reshape(1).astype(jnp.int32), sched


def flat_inverses(inverses, lanes):
    count = inverses.shape[0]
    size = inverses.shape[1] * inverses.shape[2]
    flat = jnp.pad(inverses.reshape(count, size), ((0, 0), (0, round_up(size, lanes) - size)))
    return flat.reshape(-1, lanes)


def from_partner(values, mask):
    count = lax.axis_size("yz")
    return lax.ppermute(values, "yz", [(i, i ^ mask) for i in range(count)])


def swap_pairs(near, far):
    count = lax.axis_size("gx")
    first = [(i, i ^ 1) for i in range(count) if i ^ 1 < count]
    second = [(i, i - 1 if i % 2 == 0 else i + 1) for i in range(count)]
    second = [(i, j) for i, j in second if 0 <= j < count]
    near = lax.ppermute(near, "gx", first)
    far = lax.ppermute(far, "gx", second)
    return near, far


def local(
    composition, particle_mass, mixing_rate, cell_index, section_counts, block_shuffle,
    batch_inverse, rate_exponents, stoichiometry,
):
    blocks, species, lanes = composition.shape
    reactions = rate_exponents.shape[0]
    slabs, columns = lax.axis_size("gx"), lax.axis_size("yz")
    devices = slabs * columns
    slab_cells = CELL_DEV * columns
    rows = round_up(species + 1, 8)
    steps = round_up(reactions, 8)
    slab, column = lax.axis_index("gx"), lax.axis_index("yz")
    odd = slab % 2
    place = jnp.stack([(slab - 1) * slab_cells, 2 - odd, 1 + odd]).astype(jnp.int32)

    comp = jnp.transpose(composition, (1, 0, 2))
    held = [pltpu.with_memory_space_constraint(v, pltpu.HBM) for v in (comp, particle_mass, cell_index)]
    partial = moments(place, *held, slab_cells, rows)
    near, far = partial[1], partial[2]
    near, far, own_inverse = lax.optimization_barrier((near, far, batch_inverse))
    got_near, got_far = swap_pairs(near, far)
    inverses = [own_inverse]
    for distance in range(1, slabs):
        inverses.append(lax.ppermute(own_inverse, "gx", [(i, i ^ distance) for i in range(slabs)]))
    bits = [1 << k for k in range((columns - 1).bit_length())]
    inverses = flat_inverses(jnp.concatenate(inverses, axis=0), lanes)
    own = partial[0] + got_near + got_far
    sums = own.shape[0]
    for at in range(0, len(bits), 2):
        message = jnp.concatenate([own, inverses], axis=0)
        masks = [sum(m) for m in ([bits[at]], bits[at + 1 : at + 2], bits[at : at + 2])]
        got = [from_partner(message, m) for m in (masks if at + 1 < len(bits) else masks[:1])]
        own = sum((g[:sums] for g in got), own)
        inverses = jnp.concatenate([inverses] + [g[sums:] for g in got], axis=0)
    near, far = swap_pairs(own, own)

    block_ids = jnp.arange(blocks, dtype=jnp.int32)
    slots = min(32, blocks)
    length, sched = section_schedule(section_counts, slots)
    slot = jnp.sum(
        jnp.where(block_shuffle[0][:, None] == block_ids[None, :], block_ids[:, None], 0), axis=0
    )
    batch = (slot // (blocks // devices)) ^ (slab * columns + column)
    batch = batch % columns * slabs + batch // columns
    batch = jnp.pad(batch, (0, 128))
    size = species * species
    matrices = inverses.reshape(devices, -1)[:, :size].reshape(devices, species, species)
    rates = pack_rates(rate_exponents, rows, steps)
    net = pack_net(matrices, stoichiometry, rows, steps)
    out = react(
        length, sched, batch, place, own, near, far, comp, mixing_rate, cell_index, rates, net, slots
    )
    return jnp.transpose(out, (1, 0, 2))


def solution(mesh):
    both = ("gx", "yz")
    in_specs = (
        P(both, None, None),
        P(both, None),
        P(both, None),
        P(both, None),
        P(both),
        P(both, None),
        P(both, None, None),
        P(),
        P(),
    )
    return jax.shard_map(local, mesh=mesh, in_specs=in_specs, out_specs=P(both, None, None), check_vma=False)
```
